32 devices in a mesh: frame: 4 (over z), space: 8 (over y, x, core).
Axes of the slice: x: 2, y: 2, z: 4, core: 2. Of those that a mesh axis runs over, the one named last changes fastest.
Arguments:
- latents: bfloat16 [2, 4, 512, 3072], P(None, 'frame', 'space'), may hold values from -6 to 6
- target: bfloat16 [2, 4, 512, 3072], P(None, 'frame', 'space'), may hold values from -6 to 6
- timesteps: int32 [2], replicated, may hold values from 0 to 999
- valid: int32 [2, 2], replicated, may hold values from 1 to 16, as said below
- tile_mask: int32 [2, 16, 16], replicated, may hold values from 0 to 1, as said below
- w_mod: bfloat16 [256, 18432], replicated, may hold values from -0.5 to 0.5
- w_sqkv: bfloat16 [3, 3072, 2048], P(None, None, 'space'), may hold values from -0.109375 to 0.109375
- w_sout: bfloat16 [2048, 3072], P('space'), may hold values from -0.125 to 0.125
- w_tqkv: bfloat16 [3, 3072, 2048], P(None, None, 'frame'), may hold values from -0.109375 to 0.109375
- w_tout: bfloat16 [2048, 3072], P('frame'), may hold values from -0.125 to 0.125
Outputs:
- mixed: bfloat16 [2, 4, 512, 3072], P(None, 'frame', 'space')
- loss: float32 [], replicated
The draws below stay inside these ranges and needn't reach their ends.
Inputs may be any that keep to these rules, and one draw needn't show every extreme that they name: Each video's valid frame count is 1 to 4 and valid tile count 1 to 16; video 0 is whole. `tile_mask`: entries are 0 or 1, with ones on the diagonal of every video's mask.
All inputs are finite; a program needn't handle non-finite values.
Results may differ from the reference program's by a relative error of at most 0.017.
Values may be sent and summed in bfloat16 or wider, within the bound.
A program may use at most 128 MiB of HBM per device.

```python
import math
import jax
import jax.numpy as jnp
from jax import lax

D = 3072
HEADS = 16
HEAD_DIM = 128
FREQ = 256
TILE = 32
VIDEOS = 2
SPD = 64
FRAMES = 4
SPAN = 512
TILES = 16
N_FRAME = 4
N_SPACE = 8


def draw_valid(key, part):
    counts = jax.random.randint(jax.random.fold_in(key, 11), (VIDEOS,), 1, FRAMES + 1)
    tiles = jax.random.randint(jax.random.fold_in(key, 12), (VIDEOS,), 1, TILES + 1)
    counts = counts.at[0].set(FRAMES)
    tiles = tiles.at[0].set(TILES)
    return jnp.stack([counts, tiles], 1).astype(jnp.int32)


def draw_tile_mask(key, part):
    bits = jax.random.randint(jax.random.fold_in(key, 21), (VIDEOS, TILES, TILES), 0, 2)
    diagonal = jnp.eye(TILES, dtype=jnp.int32)
    return jnp.maximum(bits, diagonal[None]).astype(jnp.int32)


def steps_of(own_key, extent, cuts, smallest, high):
    level = 1.0
    for dim, blocks in cuts:
        heights = jax.random.uniform(jax.random.fold_in(jax.random.fold_in(own_key, 6), dim), (blocks,), jnp.float32, smallest / len(cuts), high / len(cuts))
        level = level * jnp.repeat(jnp.exp(heights), extent[dim] // blocks).reshape((-1,) + (1,) * (len(extent) - 1 - dim))
    return level


def gaussian(own_key, shape, spread, reach, shards=(), kind=jnp.bfloat16):
    drawn = jax.random.normal(own_key, shape, jnp.float32) * spread
    if len(shards) > 0:
        drawn = steps_of(own_key, shape, shards, -0.22, 0.18) * drawn
    return jnp.clip(drawn, min=-reach, max=reach).astype(kind)


def setup_inputs(seed: int = 0) -> dict:
    arg_keys = jax.random.split(jax.random.key(seed), 11)
    latents = gaussian(arg_keys[0], (VIDEOS, FRAMES, SPAN, D), 1.0, 6.0, ((1, 4), (2, 8)))
    target = gaussian(arg_keys[1], (VIDEOS, FRAMES, SPAN, D), 1.0, 6.0, ((1, 4), (2, 8)))
    timesteps = jax.random.randint(arg_keys[2], (VIDEOS,), 0, 1000).astype(jnp.int32)
    valid = draw_valid(jax.random.fold_in(arg_keys[10], 71), 0)
    tile_mask = draw_tile_mask(jax.random.fold_in(arg_keys[10], 71), 0)
    w_mod = gaussian(arg_keys[5], (FREQ, 6 * D), (FREQ // 2) ** -0.5, 0.5)
    w_sqkv = gaussian(arg_keys[6], (3, D, HEADS * HEAD_DIM), D ** -0.5, 0.109375, ((2, 8),))
    w_sout = gaussian(arg_keys[7], (HEADS * HEAD_DIM, D), (HEADS * HEAD_DIM) ** -0.5, 0.125, ((0, 8),))
    w_tqkv = gaussian(arg_keys[8], (3, D, HEADS * HEAD_DIM), D ** -0.5, 0.109375, ((2, 4),))
    w_tout = gaussian(arg_keys[9], (HEADS * HEAD_DIM, D), (HEADS * HEAD_DIM) ** -0.5, 0.125, ((0, 4),))
    return {"latents": latents, "target": target, "timesteps": timesteps, "valid": valid, "tile_mask": tile_mask, "w_mod": w_mod, "w_sqkv": w_sqkv, "w_sout": w_sout, "w_tqkv": w_tqkv, "w_tout": w_tout}


def layer_norm(values):
    mean = lax.optimization_barrier(jnp.mean(values, -1, keepdims=True))
    centred = values - mean
    var = lax.optimization_barrier(jnp.mean(centred * centred, -1, keepdims=True))
    return centred * lax.rsqrt(var + 1e-06)

def time_embed(timesteps):
    half = FREQ // 2
    freqs = jnp.exp(-math.log(10000.0) * jnp.arange(half, dtype=jnp.float32) / half)
    angles = timesteps.astype(jnp.float32)[:, None] * freqs[None, :]
    return jnp.concatenate([jnp.cos(angles), jnp.sin(angles)], -1).astype(jnp.bfloat16)

def frame_attention(qkv, count, tiles, heads):
    length = qkv.shape[0]
    cols = heads * HEAD_DIM
    scale = 1.0 / math.sqrt(HEAD_DIM)
    query = jnp.transpose(qkv[:, :cols].reshape(length, heads, HEAD_DIM), (1, 0, 2))
    keys = jnp.transpose(qkv[:, cols:2 * cols].reshape(length, heads, HEAD_DIM), (1, 0, 2))
    values = jnp.transpose(qkv[:, 2 * cols:].reshape(length, heads, HEAD_DIM), (1, 0, 2))
    tile_ids = jnp.arange(length, dtype=jnp.int32) // TILE
    expanded = jnp.repeat(jnp.repeat(tiles, TILE, axis=0), TILE, axis=1)
    allowed = (expanded == 1) & (tile_ids[None, :] < count) | (tile_ids[:, None] == tile_ids[None, :])

    def one_head(parts):
        q_head, k_head, v_head = parts
        scores = jnp.dot(q_head.astype(jnp.float32), k_head.astype(jnp.float32).T) * scale
        scores = jnp.where(allowed, scores, -1e+30)
        top = lax.optimization_barrier(jnp.max(scores, -1, keepdims=True))
        weights = jnp.exp(scores - top)
        probs = (weights / lax.optimization_barrier(jnp.sum(weights, -1, keepdims=True))).astype(jnp.bfloat16)
        return jnp.dot(probs, v_head, preferred_element_type=jnp.float32).astype(jnp.bfloat16)
    outs = lax.map(one_head, (query, keys, values))
    return jnp.transpose(outs, (1, 0, 2)).reshape(length, cols)

def temporal_attention(qkv, count, heads):
    frames, places = (qkv.shape[0], qkv.shape[1])
    cols = heads * HEAD_DIM
    scale = 1.0 / math.sqrt(HEAD_DIM)
    query = qkv[..., :cols].reshape(frames, places, heads, HEAD_DIM).astype(jnp.float32)
    keys = qkv[..., cols:2 * cols].reshape(frames, places, heads, HEAD_DIM).astype(jnp.float32)
    values = qkv[..., 2 * cols:].reshape(frames, places, heads, HEAD_DIM).astype(jnp.float32)
    scores = jnp.einsum('fphd,gphd->phfg', query, keys) * scale
    frame_ids = jnp.arange(frames, dtype=jnp.int32)
    allowed = (frame_ids[None, :] < count) | (frame_ids[:, None] == frame_ids[None, :])
    scores = jnp.where(allowed, scores, -1e+30)
    top = lax.optimization_barrier(jnp.max(scores, -1, keepdims=True))
    weights = jnp.exp(scores - top)
    probs = (weights / lax.optimization_barrier(jnp.sum(weights, -1, keepdims=True))).astype(jnp.bfloat16)
    outs = jnp.einsum('phfg,gphd->fphd', probs.astype(jnp.float32), values).astype(jnp.bfloat16)
    return outs.reshape(frames, places, cols)

def group_project(attended, w_out, groups):
    rows = attended.shape[0]
    width = w_out.shape[1]
    parts = attended.reshape(rows, groups, -1).astype(jnp.float32)
    weights = w_out.reshape(groups, -1, width).astype(jnp.float32)
    terms = jnp.einsum('rgc,gcd->rgd', parts, weights).astype(jnp.bfloat16)
    return lax.optimization_barrier(jnp.sum(terms.astype(jnp.float32), axis=1))

def modulate(values, shift, scale):
    return (layer_norm(values.astype(jnp.float32)) * (1.0 + scale[:, None, None, :]) + shift[:, None, None, :]).astype(jnp.bfloat16)

def reference(latents, target, timesteps, valid, tile_mask, w_mod, w_sqkv, w_sout, w_tqkv, w_tout):
    videos, frames, span, width = latents.shape
    embed = time_embed(timesteps)
    mod = jnp.dot(embed, w_mod, preferred_element_type=jnp.float32)
    shift_one, scale_one, gate_one, shift_two, scale_two, gate_two = jnp.split(mod, 6, axis=1)
    h_one = modulate(latents, shift_one, scale_one)
    w_flat = jnp.concatenate([w_sqkv[0], w_sqkv[1], w_sqkv[2]], axis=1)
    tokens = h_one.reshape(videos * frames, span, width)
    tile_counts = jnp.repeat(valid[:, 1], frames)
    tiles = jnp.repeat(tile_mask, frames, axis=0)

    def per_frame(parts):
        frame_tokens, count, tiles_one = parts
        qkv = jnp.dot(frame_tokens, w_flat, preferred_element_type=jnp.float32).astype(jnp.bfloat16)
        attended = frame_attention(qkv, count, tiles_one, HEADS)
        return group_project(attended, w_sout, N_SPACE)
    spatial = lax.map(per_frame, (tokens, tile_counts, tiles)).reshape(videos, frames, span, width)
    x_one = (latents.astype(jnp.float32) + gate_one[:, None, None, :] * spatial).astype(jnp.bfloat16)
    h_two = modulate(x_one, shift_two, scale_two)
    blocks = span // SPD
    w_tflat = jnp.concatenate([w_tqkv[0], w_tqkv[1], w_tqkv[2]], axis=1)
    columns = h_two.reshape(videos, frames, blocks, SPD, width).transpose(0, 2, 1, 3, 4).reshape(videos * blocks, frames, SPD, width)
    frame_counts = jnp.repeat(valid[:, 0], blocks)

    def per_block(parts):
        block_tokens, count = parts
        qkv = jnp.dot(block_tokens, w_tflat, preferred_element_type=jnp.float32).astype(jnp.bfloat16)
        attended = temporal_attention(qkv, count, HEADS)
        projected = group_project(attended.reshape(frames * SPD, -1), w_tout, N_FRAME)
        return projected.reshape(frames, SPD, width)
    temporal = lax.map(per_block, (columns, frame_counts))
    temporal = temporal.reshape(videos, blocks, frames, SPD, width).transpose(0, 2, 1, 3, 4).reshape(videos, frames, span, width)
    mixed = (x_one.astype(jnp.float32) + gate_two[:, None, None, :] * temporal).astype(jnp.bfloat16)
    diff = mixed.astype(jnp.float32) - target.astype(jnp.float32)
    squares = lax.optimization_barrier(jnp.mean(diff * diff, -1))
    frame_ids = jnp.arange(frames, dtype=jnp.int32)
    tile_ids = jnp.arange(span, dtype=jnp.int32) // TILE
    mask = (frame_ids[None, :, None] < valid[:, 0][:, None, None]) & (tile_ids[None, None, :] < valid[:, 1][:, None, None])
    count = jnp.sum(valid[:, 0] * valid[:, 1]).astype(jnp.float32) * TILE
    loss = jnp.sum(jnp.where(mask, squares, 0.0)) / count
    return (mixed, loss)
```

```python
import functools
import math

import jax
import jax.numpy as jnp
from jax import lax
from jax.experimental import pallas as pl
from jax.experimental.pallas import tpu as pltpu
from jax.sharding import PartitionSpec as P

HEAD_DIM = 128
FREQ = 256
TILE = 32
ROUNDS = 2
MESH = pl.DeviceIdType.MESH
F32 = jnp.float32
BF16 = jnp.bfloat16


def norm_mod(values, shift, scale):
    mean = jnp.mean(values, -1, keepdims=True)
    centred = values - mean
    var = jnp.mean(centred * centred, -1, keepdims=True)
    return (centred * lax.rsqrt(var + 1e-06) * (1.0 + scale) + shift).astype(BF16)


def attend(query, keys, values, bias):
    scores = lax.dot_general(query, keys, (((1,), (1,)), ((), ())), preferred_element_type=F32)
    scores = scores * (1.0 / math.sqrt(HEAD_DIM)) + bias
    top = jnp.max(scores, -1, keepdims=True)
    weights = jnp.exp(scores - top)
    total = jnp.sum(weights, -1, keepdims=True)
    out = jnp.dot(weights.astype(BF16), values, preferred_element_type=F32)
    return (out * (1.0 / total)).astype(BF16)


def kernel(
    n_space, n_frame, nx, ny,
    ts_ref, valid_ref, tiles_ref, lat_hbm, wmod_hbm, wq_hbm, wso_hbm, wt_hbm, wto_hbm, tgt_hbm,
    mixed_ref, loss_ref,
    lat, tgt, MOD, G, R, H, C, x1_ref, WO, wq, wso, wt, qkv, att, att2, tqkv, A, smask, LS, LF,
    ag_s, ag_r, fw_s, fw_r, rs_s, rs_r, z_s, z_r, a_s, a_r, zw_s, zw_r, wg_s, wg_r, wf_s, wf_r,
    at_s, at_r, so_s, so_r, l_s, l_r, lf_s, lf_r, ld_sem, wm_sem,
):
    V, L, D = lat.shape
    nch = n_space // 2
    span = n_space * L
    NR = ROUNDS
    Lr, Lh, Lq = L // NR, L // 2, L // NR // 2
    sp = lax.axis_index("space")
    fr = lax.axis_index("frame")
    core = sp % 2
    chip = sp // 2
    cx, cy = chip % nx, chip // nx
    FR = wto_hbm.shape[0]
    U = FR // n_space
    sc, tc = wq.shape[2], wt.shape[2]
    sib = {"space": chip * 2 + (1 - core)}

    def chip_at(i, j):
        return ((cy + ny - j) % ny) * nx + (cx + nx - i) % nx

    def chip_to(i, j):
        return ((cy + j) % ny) * nx + (cx + i) % nx

    def rcopy(src, dst, s, r, dev):
        return pltpu.make_async_remote_copy(
            src_ref=src, dst_ref=dst, send_sem=s, recv_sem=r, device_id=dev, device_id_type=MESH
        )

    def dev_to(i, j):
        return {"space": chip_to(i, j) * 2 + core}

    chunks = wt.shape[0] * (wt.shape[1] // FREQ)
    ncol = wmod_hbm.shape[1] // tc
    mod_rounds = (ncol + chunks - 1) // chunks
    per = wt.shape[1] // FREQ

    def wm(k):
        q = k % chunks
        return pltpu.make_async_copy(
            wmod_hbm.at[:, pl.ds(k * tc, tc)],
            wt.at[q // per, pl.ds((q % per) * FREQ, FREQ)],
            wm_sem.at[q],
        )

    ld_lat = pltpu.make_async_copy(lat_hbm, lat, ld_sem.at[0])
    ld_wq = pltpu.make_async_copy(wq_hbm, wq, ld_sem.at[1])
    ld_wso = pltpu.make_async_copy(wso_hbm, wso.at[0], ld_sem.at[2])
    ld_wt = pltpu.make_async_copy(wt_hbm, wt, ld_sem.at[3])
    ld_wto = pltpu.make_async_copy(
        wto_hbm, WO.at[pl.ds(pl.multiple_of(fr * FR, FR), FR)], ld_sem.at[4]
    )
    ld_tgt = pltpu.make_async_copy(tgt_hbm, tgt, ld_sem.at[5])

    ld_lat.start()
    for k in range(min(chunks, ncol)):
        wm(k).start()
    ld_wq.start()
    ld_wso.start()
    ld_wto.start()
    ld_tgt.start()

    bar = pltpu.get_barrier_semaphore()
    for o in range(1, n_space):
        pl.semaphore_signal(bar, inc=1, device_id={"space": (sp + o) % n_space}, device_id_type=MESH)
    for o in range(1, n_frame):
        pl.semaphore_signal(bar, inc=1, device_id={"frame": (fr + o) % n_frame}, device_id_type=MESH)

    half = FREQ // 2
    lane = lax.broadcasted_iota(jnp.int32, (8, half), 1).astype(F32)
    rows8 = lax.broadcasted_iota(jnp.int32, (8, half), 0)
    steps = jnp.zeros((8, half), F32)
    for v in range(V):
        steps = jnp.where(rows8 == v, ts_ref[v].astype(F32), steps)
    angles = steps * jnp.exp(-math.log(10000.0) * lane / half)
    embed = jnp.concatenate([jnp.cos(angles), jnp.sin(angles)], -1).astype(BF16)

    def mod_chunk(k):
        q = k % chunks
        w = wt[q // per, pl.ds((q % per) * FREQ, FREQ), :]
        sec, col = (k * tc) // D, (k * tc) % D
        MOD[sec, :, col : col + tc] = jnp.dot(embed, w, preferred_element_type=F32)

    def mod(v, i):
        return MOD[i, v : v + 1, :]

    def send2(blk, ss, rs, h, i, j):
        if h == 0:
            src = blk(chip, 0) if j == 0 else blk(chip_at(i, 0), 0)
            dev = dev_to(i, 0) if j == 0 else dev_to(0, j)
        else:
            src = blk(chip, 1) if i == 0 else blk(chip_at(0, j), 1)
            dev = dev_to(0, j) if i == 0 else dev_to(i, 0)
        return rcopy(src, src, ss, rs, dev)

    def recv2(blk, ss, rs, h, i, j):
        slot = blk(chip_at(i, j), h)
        return rcopy(slot, slot, ss, rs, sib)

    OFFS = [(i, j) for j in range(ny) for i in range(nx)]
    OWN_SENDS = []
    for i in range(1, nx):
        OWN_SENDS.append((0, i, 0))
    for j in range(1, ny):
        OWN_SENDS.append((1, 0, j))
    for j in range(1, ny):
        OWN_SENDS.append((0, 0, j))
    for i in range(1, nx):
        OWN_SENDS.append((1, i, 0))
    FIRST = [(0, i, 0) for i in range(1, nx)] + [(1, 0, j) for j in range(1, ny)]

    def relays_of(h, i, j):
        if h == 0:
            return [(0, i, jj) for jj in range(1, ny)]
        return [(1, ii, j) for ii in range(1, nx)]

    SECOND = [(0, 0, j) for j in range(1, ny)] + [(1, i, 0) for i in range(1, nx)]
    THIRD = [(h, i, j) for h in range(2) for j in range(1, ny) for i in range(1, nx)]
    ALL = [(h, i, j) for h in range(2) for (i, j) in OFFS if (i, j) != (0, 0)]

    def tok(v):
        return lambda c, h: G.at[v, c, core, pl.ds(h * Lh, Lh)]

    def ag(v, h, i, j):
        return send2(tok(v), ag_s.at[v, h, i, j], ag_r.at[v, h, i, j], h, i, j)

    def ag_in(v, h, i, j):
        return recv2(tok(v), ag_s.at[v, h, i, j], ag_r.at[v, h, i, j], h, i, j)

    def fw(v, h, i, j):
        slot = G.at[v, chip_at(i, j), core, pl.ds(h * Lh, Lh)]
        return rcopy(slot, slot, fw_s.at[v, h, i, j], fw_r.at[v, h, i, j], sib)

    def fw_in(v, h, i, j):
        slot = G.at[v, chip_at(i, j), 1 - core, pl.ds(h * Lh, Lh)]
        return rcopy(slot, slot, fw_s.at[v, h, i, j], fw_r.at[v, h, i, j], sib)

    def unit(f, s, h):
        row = pl.multiple_of(f * FR + s * U, U)
        return WO.at[pl.ds(row, U), pl.ds(h * (D // 2), D // 2)]

    def wrow(o):
        return lambda c, h: unit((fr + o) % n_frame, c * 2 + core, h)

    def wg(o, h, i, j):
        return send2(wrow(o), wg_s.at[o, h, i, j], wg_r.at[o, h, i, j], h, i, j)

    def wg_in(o, h, i, j):
        return recv2(wrow(o), wg_s.at[o, h, i, j], wg_r.at[o, h, i, j], h, i, j)

    def wf(o, h, i, j):
        slot = unit((fr + o) % n_frame, chip_at(i, j) * 2 + core, h)
        return rcopy(slot, slot, wf_s.at[o, h, i, j], wf_r.at[o, h, i, j], sib)

    def wf_in(o, h, i, j):
        slot = unit((fr + o) % n_frame, chip_at(i, j) * 2 + 1 - core, h)
        return rcopy(slot, slot, wf_s.at[o, h, i, j], wf_r.at[o, h, i, j], sib)

    def piece(r, h):
        return pl.ds(r * Lr + h * Lq, Lq)

    def rs(v, r, h, i, j, first):
        src = G.at[v, chip_to(i, j), core, piece(r, h)]
        if h == 0:
            dev = dev_to(i, 0) if first else dev_to(0, j)
        else:
            dev = dev_to(0, j) if first else dev_to(i, 0)
        return rcopy(
            src, R.at[v, r, h, i, j], rs_s.at[v, r, h, i, j], rs_r.at[v, r, h, i, j], dev
        )

    def rs_first(h):
        if h == 0:
            far = [(i, j) for i in range(1, nx) for j in range(1, ny)]
            near = [(i, 0) for i in range(1, nx)]
        else:
            far = [(i, j) for j in range(1, ny) for i in range(1, nx)]
            near = [(0, j) for j in range(1, ny)]
        return far, near

    def hblk(v, r, f):
        return H.at[v, f, pl.ds(r * Lr, Lr)]

    def zsend(v, r, d, s):
        f = fr - s if d == 0 else fr + s
        to = fr + 1 if d == 0 else fr - 1
        blk = hblk(v, r, f)
        return rcopy(blk, blk, z_s.at[v, r, d, s], z_r.at[v, r, d, s + 1], {"frame": to})

    def zin(v, r, d, s):
        f = fr - s if d == 0 else fr + s
        blk = hblk(v, r, f)
        return rcopy(blk, blk, z_s.at[v, r, d, s], z_r.at[v, r, d, s], sib)

    def wunit(f):
        return WO.at[pl.ds(pl.multiple_of(f * FR + sp * U, U), U)]

    def zwsend(d, s):
        f = fr - s if d == 0 else fr + s
        to = fr + 1 if d == 0 else fr - 1
        src = wto_hbm.at[pl.ds(pl.multiple_of(sp * U, U), U)] if s == 0 else wunit(f)
        return rcopy(src, wunit(f), zw_s.at[d, s], zw_r.at[d, s + 1], {"frame": to})

    def zwin(d, s):
        f = fr - s if d == 0 else fr + s
        return rcopy(wunit(f), wunit(f), zw_s.at[d, s], zw_r.at[d, s], sib)

    def has(d, s):
        return fr >= s if d == 0 else fr + s < n_frame

    def sends(d, s):
        if d == 0:
            return (fr >= s) & (fr + 1 < n_frame)
        return (fr + s < n_frame) & (fr >= 1)

    def line_step(send, arrive, s):
        for d in range(2):
            if s > 0:
                pl.when(has(d, s))(lambda d=d: arrive(d, s).wait_recv())
            if s < n_frame - 1:
                pl.when(sends(d, s))(lambda d=d: send(d, s).start())

    def line_end(send):
        for s in range(n_frame - 1):
            for d in range(2):
                pl.when(sends(d, s))(lambda d=d, s=s: send(d, s).wait_send())

    def zstep(v, r, s):
        line_step(functools.partial(zsend, v, r), functools.partial(zin, v, r), s)

    def zwstep(s):
        line_step(zwsend, zwin, s)

    def ax(v, r, o):
        cols = pl.ds(pl.multiple_of(fr * tc, tc), tc)
        dst = (fr + o) % n_frame
        rows = pl.ds(r * Lr, Lr)
        return rcopy(
            A.at[v, dst, rows], C.at[v, rows, cols], a_s.at[v, r, o], a_r.at[v, r, o], {"frame": dst}
        )

    def ax_in(v, r, o):
        src = (fr + n_frame - o) % n_frame
        cols = pl.ds(pl.multiple_of(src * tc, tc), tc)
        rows = pl.ds(r * Lr, Lr)
        return rcopy(
            A.at[v, src, rows], C.at[v, rows, cols], a_s.at[v, r, o], a_r.at[v, r, o], {"frame": src}
        )

    def attx(v):
        return rcopy(att.at[v, :, 1 - core], att2.at[v], at_s.at[v], at_r.at[v], sib)

    wso_x = rcopy(wso_hbm, wso.at[1], so_s.at[0], so_r.at[0], sib)

    def ls(o):
        return rcopy(LS.at[sp], LS.at[sp], l_s.at[o], l_r.at[o], {"space": (sp + o) % n_space})

    def ls_in(o):
        slot = LS.at[(sp + n_space - o) % n_space]
        return rcopy(slot, slot, l_s.at[o], l_r.at[o], {"space": (sp + o) % n_space})

    def lf(o):
        return rcopy(LF.at[fr], LF.at[fr], lf_s.at[o], lf_r.at[o], {"frame": (fr + o) % n_frame})

    def lf_in(o):
        slot = LF.at[(fr + n_frame - o) % n_frame]
        return rcopy(slot, slot, lf_s.at[o], lf_r.at[o], {"frame": (fr + o) % n_frame})

    def first_norm(v):
        G[v, chip, core] = norm_mod(lat[v].astype(F32), mod(v, 0), mod(v, 1))

    def masks():
        nt = tiles_ref.shape[1]
        qt = lax.broadcasted_iota(jnp.int32, (nt, nt), 0)
        kt = lax.broadcasted_iota(jnp.int32, (nt, nt), 1)
        ids = (
            lax.broadcasted_iota(jnp.int32, (span, nt), 0) // TILE
            == lax.broadcasted_iota(jnp.int32, (span, nt), 1)
        ).astype(BF16)
        for v in range(V):
            ok = ((tiles_ref[v] == 1) & (kt < valid_ref[v, 1])) | (qt == kt)
            rows = jnp.dot(ids, ok.astype(BF16), preferred_element_type=F32).astype(BF16)
            full = lax.dot_general(rows, ids, (((1,), (1,)), ((), ())), preferred_element_type=F32)
            smask[v] = jnp.where(full > 0.5, 0.0, -1e30).astype(BF16)

    QB = 256

    def spatial_qkv(v):
        mt = 256 // (2 * L)
        nm = nch // mt

        def step(i, _):
            j, m = i // nm, i % nm
            x = G[v, pl.ds(m * mt, mt)].reshape(256, D)
            qkv[j, pl.ds(pl.multiple_of(m * 256, 256), 256), :] = jnp.dot(
                x, wq[j], preferred_element_type=F32
            ).astype(BF16)
            return 0

        lax.fori_loop(0, 3 * nm, step, 0)

    def spatial_att(v):
        mt = QB // (2 * L)
        for h in range(sc // HEAD_DIM):
            hs = slice(h * HEAD_DIM, (h + 1) * HEAD_DIM)

            def step(i, _):
                rows = pl.ds(pl.multiple_of(i * QB, QB), QB)
                out = attend(
                    qkv[0, rows, hs], qkv[1, :, hs], qkv[2, :, hs], smask[v, rows, :].astype(F32)
                )
                att[v, pl.ds(i * mt, mt), :, :, hs] = out.reshape(mt, 2, L, HEAD_DIM)
                return 0

            lax.fori_loop(0, span // QB, step, 0)

    CB = 512

    def spatial_out(v):
        def step(i, _):
            cols = pl.ds(pl.multiple_of(i * CB, CB), CB)
            mine = att[v, :, core].reshape(nch * L, sc)
            other = att2[v].reshape(nch * L, sc)
            t = jnp.dot(mine, wso[0, :, cols], preferred_element_type=F32)
            t = t + jnp.dot(other, wso[1, :, cols], preferred_element_type=F32)
            G[v, :, core, :, cols] = t.astype(BF16).reshape(nch, L, CB)
            return 0

        lax.fori_loop(0, D // CB, step, 0)

    def rs_start(v, r):
        for k in range(2):
            for h in range(2):
                for i, j in rs_first(h)[k]:
                    rs(v, r, h, i, j, True).start()

    def rs_relay(v, r):
        for h in range(2):
            for b in range(1, ny if h == 0 else nx):
                if h == 0:
                    srcs, i, j = [(i, b) for i in range(1, nx)], 0, b
                else:
                    srcs, i, j = [(b, j) for j in range(1, ny)], b, 0
                c = chip_to(i, j)
                total = G[v, c, core, piece(r, h)].astype(F32)
                for a in srcs:
                    rs(v, r, h, a[0], a[1], True).wait_recv()
                    total = total + R[v, r, h, a[0], a[1]].astype(F32)
                G[v, c, core, piece(r, h)] = total.astype(BF16)
                rs(v, r, h, i, j, False).start()

    def finish(v, r):
        for h in range(2):
            rows = piece(r, h)
            so = G[v, chip, core, rows].astype(F32)
            if h == 0:
                order = [(i, 0) for i in range(1, nx)] + [(0, j) for j in range(1, ny)]
            else:
                order = [(0, j) for j in range(1, ny)] + [(i, 0) for i in range(1, nx)]
            for i, j in order:
                rs(v, r, h, i, j, True).wait_recv()
                so = so + R[v, r, h, i, j].astype(F32)
            x1 = (lat[v, rows].astype(F32) + mod(v, 2) * so).astype(BF16)
            x1_ref[v, rows] = x1
            H[v, fr, rows] = norm_mod(x1.astype(F32), mod(v, 3), mod(v, 4))
        zstep(v, r, 0)

    def rs_end(v):
        for r in range(NR):
            for h in range(2):
                for i, j in OFFS:
                    if (i, j) != (0, 0):
                        rs(v, r, h, i, j, True).wait_send()

    def temporal(v, r):
        NB = 256
        nn = tc // NB
        tl = n_frame * Lr

        def step(i, _):
            j, n = i // nn, i % nn
            cols = pl.ds(pl.multiple_of(n * NB, NB), NB)
            x = H[v, :, r * Lr : (r + 1) * Lr, :].reshape(tl, D)
            tqkv[j, :, cols] = jnp.dot(x, wt[j, :, cols], preferred_element_type=F32).astype(BF16)
            return 0

        lax.fori_loop(0, 3 * nn, step, 0)
        q = lax.broadcasted_iota(jnp.int32, (tl, tl), 0)
        k = lax.broadcasted_iota(jnp.int32, (tl, tl), 1)
        ok = (q % Lr == k % Lr) & ((k // Lr < valid_ref[v, 0]) | (q // Lr == k // Lr))
        bias = jnp.where(ok, 0.0, -1e30)
        for h in range(tc // HEAD_DIM):
            hs = slice(h * HEAD_DIM, (h + 1) * HEAD_DIM)
            out = attend(tqkv[0, :, hs], tqkv[1, :, hs], tqkv[2, :, hs], bias)
            A[v, :, r * Lr : (r + 1) * Lr, hs] = out.reshape(n_frame, Lr, HEAD_DIM)
        for o in range(1, n_frame):
            ax(v, r, o).start()
        rows = slice(r * Lr, (r + 1) * Lr)
        C[v, rows, pl.ds(pl.multiple_of(fr * tc, tc), tc)] = A[v, fr, rows]

    for k in range(min(chunks, ncol)):
        wm(k).wait()
        mod_chunk(k)
        if (k + 1) * tc == 2 * D:
            ld_lat.wait()
            first_norm(0)
            pl.semaphore_wait(bar, (n_space - 1) + (n_frame - 1))
            for t in OWN_SENDS:
                ag(0, *t).start()
            zwstep(0)
            for h in range(2):
                fw(0, h, 0, 0).start()
            wso_x.start()
    for m in range(1, mod_rounds):
        ks = range(m * chunks, min((m + 1) * chunks, ncol))
        for k in ks:
            wm(k).start()
        for k in ks:
            wm(k).wait()
            mod_chunk(k)
    ld_wt.start()
    first_norm(1)

    def gather_first(v):
        for h, i, j in FIRST:
            ag_in(v, h, i, j).wait_recv()
            for t in relays_of(h, i, j):
                ag(v, *t).start()
            fw(v, h, i, j).start()

    def gather_rest(v):
        for h, i, j in SECOND + THIRD:
            ag_in(v, h, i, j).wait_recv()
            fw(v, h, i, j).start()

    def gather_own(v):
        for t in OWN_SENDS:
            ag(v, *t).start()
        for h in range(2):
            fw(v, h, 0, 0).start()

    def gather_end(v):
        for t in ALL:
            ag(v, *t).wait_send()
        for h in range(2):
            for i, j in OFFS:
                fw(v, h, i, j).wait_send()

    def spatial(v, between=None):
        for h in range(2):
            for i, j in OFFS:
                fw_in(v, h, i, j).wait_recv()
        if v == 0:
            ld_wq.wait()
        spatial_qkv(v)
        spatial_att(v)
        attx(v).start()
        if between is not None:
            between()
        gather_end(v)
        if v == 0:
            ld_wso.wait()
            wso_x.wait_recv()
        attx(v).wait_recv()
        spatial_out(v)
        for r in range(NR):
            rs_start(v, r)

    def weights_own(o):
        for t in OWN_SENDS:
            wg(o, *t).start()
        for h in range(2):
            wf(o, h, 0, 0).start()

    def weights_first(o):
        for h, i, j in FIRST:
            wg_in(o, h, i, j).wait_recv()
            for t in relays_of(h, i, j):
                wg(o, *t).start()
            wf(o, h, i, j).start()

    def weights_rest(o):
        for h, i, j in SECOND + THIRD:
            wg_in(o, h, i, j).wait_recv()
            wf(o, h, i, j).start()

    masks()
    gather_first(0)
    gather_own(1)
    zwstep(1)
    gather_rest(0)
    spatial(0, lambda: [zwstep(s) for s in range(2, n_frame)])
    for r in range(NR):
        rs_relay(0, r)
    gather_first(1)
    for r in range(NR):
        finish(0, r)
    gather_rest(1)
    weights_own(1)
    for r in range(NR):
        zstep(0, r, 1)
    spatial(1)
    for s in range(2, n_frame):
        for r in range(NR):
            zstep(0, r, s)
            if s == 2:
                rs_relay(1, r)
        if s == 2:
            weights_first(1)
            for r in range(NR):
                finish(1, r)
            for o in range(2, n_frame):
                weights_own(o)
            weights_rest(1)
    if n_frame <= 2:
        raise ValueError("frames")
    ld_wt.wait()
    for r in range(NR):
        temporal(0, r)
    for r in range(NR):
        zstep(1, r, 1)
    for o in range(2, n_frame):
        weights_first(o)
        weights_rest(o)
        if o < n_frame:
            for r in range(NR):
                zstep(1, r, o)
    for r in range(NR):
        temporal(1, r)

    for o in range(1, n_frame):
        for h in range(2):
            for i, j in OFFS:
                wf_in(o, h, i, j).wait_recv()
    for v in range(V):
        for r in range(NR):
            for o in range(1, n_frame):
                ax_in(v, r, o).wait_recv()
    ld_tgt.wait()
    ld_wto.wait()

    def out_step(i, total):
        cols = pl.ds(pl.multiple_of(i * CB, CB), CB)
        a = C[...].reshape(V * L, n_frame * tc)
        acc = jnp.dot(a, WO[:, cols], preferred_element_type=F32)
        part = []
        for v in range(V):
            gate = MOD[5, v : v + 1, cols]
            m = x1_ref[v, :, cols].astype(F32) + gate * acc[v * L : (v + 1) * L]
            m = m.astype(BF16)
            mixed_ref[v, :, cols] = m
            diff = m.astype(F32) - tgt[v, :, cols].astype(F32)
            part.append(jnp.sum(diff * diff, -1, keepdims=True))
        return total + jnp.concatenate(part, 0)

    squares = lax.fori_loop(0, D // CB, out_step, jnp.zeros((V * L, 1), F32)) * (1.0 / D)
    place = sp * L + lax.broadcasted_iota(jnp.int32, (L, 1), 0)
    here = jnp.zeros((1, 1), F32)
    count = jnp.int32(0)
    for v in range(V):
        keep = (place // TILE < valid_ref[v, 1]) & (fr < valid_ref[v, 0])
        here = here + jnp.sum(
            jnp.where(keep, squares[v * L : (v + 1) * L], 0.0), 0, keepdims=True
        )
        count = count + valid_ref[v, 0] * valid_ref[v, 1]
    LS[sp] = jnp.broadcast_to(here, (8, 128))
    for o in range(1, n_space):
        ls(o).start()
    for o in range(1, n_space):
        ls_in(o).wait_recv()
    LF[fr] = jnp.sum(LS[...], 0)
    for o in range(1, n_frame):
        lf(o).start()
    for o in range(1, n_frame):
        lf_in(o).wait_recv()
    loss_ref[...] = jnp.sum(LF[...], 0) / (count.astype(F32) * TILE)

    wso_x.wait_send()
    for v in range(V):
        attx(v).wait_send()
        rs_end(v)
        for r in range(NR):
            line_end(functools.partial(zsend, v, r))
            for o in range(1, n_frame):
                ax(v, r, o).wait_send()
    line_end(zwsend)
    for o in range(1, n_frame):
        lf(o).wait_send()
        for t in ALL:
            wg(o, *t).wait_send()
        for h in range(2):
            for i, j in OFFS:
                wf(o, h, i, j).wait_send()
    for o in range(1, n_space):
        ls(o).wait_send()


def run_kernel(timesteps, valid, tile_mask, latents, w_mod, w_sqkv, w_sout, w_tqkv, w_tout, target):
    V, L, D = latents.shape
    n_space = lax.axis_size("space")
    n_frame = lax.axis_size("frame")
    nch = n_space // 2
    ny = 2 if nch % 2 == 0 else 1
    nx = nch // ny
    NR = ROUNDS
    sc, tc = w_sqkv.shape[2], w_tqkv.shape[2]
    span = n_space * L
    tl = n_frame * L // NR
    dma = pltpu.SemaphoreType.DMA
    vm = pl.BlockSpec(memory_space=pltpu.VMEM)
    sm = pl.BlockSpec(memory_space=pltpu.SMEM)
    hbm = pl.BlockSpec(memory_space=pl.ANY)
    chunks = 3 * (D // FREQ)
    return pl.pallas_call(
        functools.partial(kernel, n_space, n_frame, nx, ny),
        out_shape=(
            jax.ShapeDtypeStruct((V, L, D), BF16),
            jax.ShapeDtypeStruct((8, 128), F32),
        ),
        in_specs=[sm, sm, vm] + [hbm] * 7,
        out_specs=(vm, vm),
        scratch_shapes=[
            pltpu.VMEM((V, L, D), BF16),
            pltpu.VMEM((V, L, D), BF16),
            pltpu.VMEM((6, 8, D), F32),
            pltpu.VMEM((V, nch, 2, L, D), BF16),
            pltpu.VMEM((V, NR, 2, nx, ny, L // NR // 2, D), BF16),
            pltpu.VMEM((V, n_frame, L, D), BF16),
            pltpu.VMEM((V, L, n_frame * tc), BF16),
            pltpu.VMEM((V, L, D), BF16),
            pltpu.VMEM((n_frame * w_tout.shape[0], D), BF16),
            pltpu.VMEM(w_sqkv.shape, BF16),
            pltpu.VMEM((2,) + w_sout.shape, BF16),
            pltpu.VMEM(w_tqkv.shape, BF16),
            pltpu.VMEM((3, span, sc), BF16),
            pltpu.VMEM((V, nch, 2, L, sc), BF16),
            pltpu.VMEM((V, nch, L, sc), BF16),
            pltpu.VMEM((3, tl, tc), BF16),
            pltpu.VMEM((V, n_frame, L, tc), BF16),
            pltpu.VMEM((V, span, span), BF16),
            pltpu.VMEM((n_space, 8, 128), F32),
            pltpu.VMEM((n_frame, 8, 128), F32),
            dma((V, 2, nx, ny)), dma((V, 2, nx, ny)), dma((V, 2, nx, ny)), dma((V, 2, nx, ny)),
            dma((V, NR, 2, nx, ny)), dma((V, NR, 2, nx, ny)),
            dma((V, NR, 2, n_frame)), dma((V, NR, 2, n_frame)),
            dma((V, NR, n_frame)), dma((V, NR, n_frame)),
            dma((2, n_frame)), dma((2, n_frame)),
            dma((n_frame, 2, nx, ny)), dma((n_frame, 2, nx, ny)),
            dma((n_frame, 2, nx, ny)), dma((n_frame, 2, nx, ny)),
            dma((V,)), dma((V,)), dma((1,)), dma((1,)),
            dma((n_space,)), dma((n_space,)), dma((n_frame,)), dma((n_frame,)),
            dma((6,)), dma((chunks,)),
        ],
        compiler_params=pltpu.CompilerParams(
            collective_id=0, has_side_effects=True, vmem_limit_bytes=60 * 1024 * 1024
        ),
        cost_estimate=pl.CostEstimate(
            flops=14_000_000_000, bytes_accessed=35_000_000, transcendentals=3_000_000
        ),
        name="block",
    )(timesteps, valid, tile_mask, latents, w_mod, w_sqkv, w_sout, w_tqkv, w_tout, target)


def shards(latents, target, timesteps, valid, tile_mask, w_mod, w_sqkv, w_sout, w_tqkv, w_tout):
    videos, frames_dev, span_dev, width = latents.shape
    shape = (videos, span_dev, width)
    mixed, loss = run_kernel(
        timesteps, valid, tile_mask, latents.reshape(shape), w_mod,
        w_sqkv, w_sout, w_tqkv, w_tout, target.reshape(shape),
    )
    return (mixed.reshape(latents.shape), loss[0, 0])


def solution(mesh):
    return jax.shard_map(
        shards,
        mesh=mesh,
        in_specs=(
            P(None, "frame", "space", None),
            P(None, "frame", "space", None),
            P(),
            P(),
            P(),
            P(),
            P(None, None, "space"),
            P("space", None),
            P(None, None, "frame"),
            P("frame", None),
        ),
        out_specs=(P(None, "frame", "space", None), P()),
        check_vma=False,
    )
```

```python
import functools
import math

import jax
import jax.numpy as jnp
from jax import lax
from jax.experimental import pallas as pl
from jax.experimental.pallas import tpu as pltpu
from jax.sharding import PartitionSpec as P

HEAD_DIM = 128
FREQ = 256
TILE = 32
ROUNDS = ((0, 4), (4, 4), (8, 8))
UNITS = 2
MESH = pl.DeviceIdType.MESH
F32 = jnp.float32
BF16 = jnp.bfloat16


def norm_mod(values, shift, scale):
    mean = jnp.mean(values, -1, keepdims=True)
    centred = values - mean
    var = jnp.mean(centred * centred, -1, keepdims=True)
    return (centred * lax.rsqrt(var + 1e-06) * (1.0 + scale) + shift).astype(BF16)


def attend(query, keys, values, bias):
    scores = lax.dot_general(query, keys, (((1,), (1,)), ((), ())), preferred_element_type=F32)
    scores = scores * (1.0 / math.sqrt(HEAD_DIM)) + bias
    top = jnp.max(scores, -1, keepdims=True)
    weights = jnp.exp(scores - top)
    total = jnp.sum(weights, -1, keepdims=True)
    out = jnp.dot(weights.astype(BF16), values, preferred_element_type=F32)
    return (out * (1.0 / total)).astype(BF16)


def kernel(
    n_space, n_frame, nx, ny,
    ts_ref, valid_ref, tiles_ref, lat_hbm, wmod_hbm, wq_hbm, wso_hbm, wt_hbm, wto_hbm, tgt_hbm,
    mixed_ref, loss_ref,
    lat, tgt, MOD, G, X, R, H, C, x1_ref, WO, wq, wso, wt, qkv, att, att2, tqkv, A, smask, LS,
    ag_s, ag_r, fw_s, fw_r, rs_s, rs_r, z_s, z_r, a_s, a_r, zw_s, zw_r, wg_s, wg_r, wf_s, wf_r,
    at_s, at_r, so_s, so_r, l_s, l_r, ld_sem, own_sem, wm_sem,
):
    V, L, D = lat.shape
    nch = n_space // 2
    span = n_space * L
    NR = len(ROUNDS)
    NU = UNITS
    Lu, Lh, Dh = L // NU, L // 2, D // 2
    sp = lax.axis_index("space")
    fr = lax.axis_index("frame")
    core = sp % 2
    chip = sp // 2
    cx, cy = chip % nx, chip // nx
    FR = wto_hbm.shape[0]
    U = FR // n_space
    sc, tc = wq.shape[2], wt.shape[2]
    sib = {"space": chip * 2 + (1 - core)}

    def chip_at(i, j):
        return ((cy + ny - j) % ny) * nx + (cx + nx - i) % nx

    def chip_to(i, j):
        return ((cy + j) % ny) * nx + (cx + i) % nx

    def at(i, j):
        return j * nx + i - 1

    def drain(ref, sem):
        pltpu.make_async_copy(ref, ref, sem).wait()

    def rcopy(src, dst, s, r, dev):
        return pltpu.make_async_remote_copy(
            src_ref=src, dst_ref=dst, send_sem=s, recv_sem=r, device_id=dev, device_id_type=MESH
        )

    def dev_to(i, j):
        return {"space": chip_to(i, j) * 2 + core}

    chunks = wt.shape[0] * (wt.shape[1] // FREQ)
    ncol = wmod_hbm.shape[1] // tc
    mod_rounds = (ncol + chunks - 1) // chunks
    per = wt.shape[1] // FREQ

    def wm(k):
        q = k % chunks
        return pltpu.make_async_copy(
            wmod_hbm.at[:, pl.ds(k * tc, tc)],
            wt.at[q // per, pl.ds((q % per) * FREQ, FREQ)],
            wm_sem.at[q // per],
        )

    ld_lat = pltpu.make_async_copy(lat_hbm, lat, ld_sem.at[0])
    ld_wq = pltpu.make_async_copy(wq_hbm, wq, ld_sem.at[1])
    ld_wso = pltpu.make_async_copy(wso_hbm, wso.at[0], ld_sem.at[2])
    ld_wt = pltpu.make_async_copy(wt_hbm, wt, ld_sem.at[3])
    ld_wto = pltpu.make_async_copy(
        wto_hbm, WO.at[pl.ds(pl.multiple_of(fr * FR, FR), FR)], ld_sem.at[4]
    )
    ld_tgt = pltpu.make_async_copy(tgt_hbm, tgt, ld_sem.at[5])

    bar = pltpu.get_barrier_semaphore()
    for o in range(1, n_space * n_frame):
        to = (fr * n_space + sp + o) % (n_space * n_frame)
        pl.semaphore_signal(
            bar, inc=1, device_id={"frame": to // n_space, "space": to % n_space}, device_id_type=MESH
        )

    half = FREQ // 2
    lane = lax.broadcasted_iota(jnp.int32, (8, half), 1).astype(F32)
    rows8 = lax.broadcasted_iota(jnp.int32, (8, half), 0)
    steps = jnp.zeros((8, half), F32)
    for v in range(V):
        steps = jnp.where(rows8 == v, ts_ref[v].astype(F32), steps)
    angles = steps * jnp.exp(-math.log(10000.0) * lane / half)
    embed = jnp.concatenate([jnp.cos(angles), jnp.sin(angles)], -1).astype(BF16)

    def mod_chunk(k):
        q = k % chunks
        w = wt[q // per, pl.ds((q % per) * FREQ, FREQ), :]
        sec, col = (k * tc) // D, (k * tc) % D
        MOD[sec, :, col : col + tc] = jnp.dot(embed, w, preferred_element_type=F32)

    def mod(v, i):
        return MOD[i, v : v + 1, :]

    def send2(blk, ss, rs, h, i, j):
        if h == 0:
            src = blk(chip, 0) if j == 0 else blk(chip_at(i, 0), 0)
            dev = dev_to(i, 0) if j == 0 else dev_to(0, j)
        else:
            src = blk(chip, 1) if i == 0 else blk(chip_at(0, j), 1)
            dev = dev_to(0, j) if i == 0 else dev_to(i, 0)
        return rcopy(src, src, ss, rs, dev)

    def recv2(blk, ss, rs, h, i, j):
        slot = blk(chip_at(i, j), h)
        return rcopy(slot, slot, ss, rs, sib)

    OFFS = [(i, j) for j in range(ny) for i in range(nx)]
    FIRST = [(0, i, 0) for i in range(1, nx)] + [(1, 0, j) for j in range(1, ny)]

    def relays_of(h, i, j):
        if h == 0:
            return [(0, i, jj) for jj in range(1, ny)]
        return [(1, ii, j) for ii in range(1, nx)]

    SECOND = [(0, 0, j) for j in range(1, ny)] + [(1, i, 0) for i in range(1, nx)]
    OWN_SENDS = FIRST + SECOND
    THIRD = [(h, i, j) for h in range(2) for j in range(1, ny) for i in range(1, nx)]
    ALL = [(h, i, j) for h in range(2) for (i, j) in OFFS if (i, j) != (0, 0)]

    def tok(v):
        return lambda c, h: G.at[v, c, core, pl.ds(h * Lh, Lh)]

    def ag(v, h, i, j):
        return send2(tok(v), ag_s.at[v], ag_r.at[v, h, at(i, j)], h, i, j)

    def ag_in(v, h, i, j):
        return recv2(tok(v), ag_s.at[v], ag_r.at[v, h, at(i, j)], h, i, j)

    def fw(v, h, i, j):
        slot = G.at[v, chip_at(i, j), core, pl.ds(h * Lh, Lh)]
        return rcopy(slot, slot, fw_s.at[v], fw_r.at[v, min(j, 1)], sib)

    def unit(f, s, h):
        row = pl.multiple_of(f * FR + s * U, U)
        return WO.at[pl.ds(row, U), pl.ds(h * (D // 2), D // 2)]

    def wrow(o):
        return lambda c, h: unit((fr + o) % n_frame, c * 2 + core, h)

    def wg(o, h, i, j):
        return send2(wrow(o), wg_s.at[0], wg_r.at[o - 1, h, at(i, j)], h, i, j)

    def wg_in(o, h, i, j):
        return recv2(wrow(o), wg_s.at[0], wg_r.at[o - 1, h, at(i, j)], h, i, j)

    def wf(o, h, i, j):
        slot = unit((fr + o) % n_frame, chip_at(i, j) * 2 + core, h)
        return rcopy(slot, slot, wf_s.at[0], wf_r.at[0], sib)

    def piece(r):
        a, n = ROUNDS[r]
        return pl.ds(a * L // 16, n * L // 16)

    def side(h):
        return pl.ds(h * Dh, Dh)

    def rs(v, r, h, i, j, first):
        src = G.at[v, chip_to(i, j), core, piece(r), side(h)]
        if h == 0:
            dev = dev_to(i, 0) if first else dev_to(0, j)
        else:
            dev = dev_to(0, j) if first else dev_to(i, 0)
        return rcopy(
            src, R.at[v, h, at(i, j), piece(r)], rs_s.at[v], rs_r.at[v, r, h, at(i, j)], dev
        )

    def rs_first(h):
        if h == 0:
            far = [(i, j) for i in range(1, nx) for j in range(1, ny)]
            near = [(i, 0) for i in range(1, nx)]
        else:
            far = [(i, j) for j in range(1, ny) for i in range(1, nx)]
            near = [(0, j) for j in range(1, ny)]
        return far, near

    def hblk(v, r, f):
        return H.at[v, f, piece(r)]

    def zsend(v, r, d, s):
        f = fr - s if d == 0 else fr + s
        to = fr + 1 if d == 0 else fr - 1
        blk = hblk(v, r, f)
        return rcopy(blk, blk, z_s.at[v, r, d, s], z_r.at[v, r, d, s], {"frame": to})

    def zin(v, r, d, s):
        f = fr - s if d == 0 else fr + s
        blk = hblk(v, r, f)
        return rcopy(blk, blk, z_s.at[v, r, d, s - 1], z_r.at[v, r, d, s - 1], sib)

    def wunit(f):
        return WO.at[pl.ds(pl.multiple_of(f * FR + sp * U, U), U)]

    def zwsend(d, s):
        f = fr - s if d == 0 else fr + s
        to = fr + 1 if d == 0 else fr - 1
        src = wto_hbm.at[pl.ds(pl.multiple_of(sp * U, U), U)] if s == 0 else wunit(f)
        return rcopy(src, wunit(f), zw_s.at[d, s], zw_r.at[d, s], {"frame": to})

    def zwin(d, s):
        f = fr - s if d == 0 else fr + s
        return rcopy(wunit(f), wunit(f), zw_s.at[d, s - 1], zw_r.at[d, s - 1], sib)

    def has(d, s):
        return fr >= s if d == 0 else fr + s < n_frame

    def sends(d, s):
        if d == 0:
            return (fr >= s) & (fr + 1 < n_frame)
        return (fr + s < n_frame) & (fr >= 1)

    def line_step(send, arrive, s):
        for d in range(2):
            if s > 0:
                pl.when(has(d, s))(lambda d=d: arrive(d, s).wait_recv())
            if s < n_frame - 1:
                pl.when(sends(d, s))(lambda d=d: send(d, s).start())

    def line_end(send):
        for s in range(n_frame - 1):
            for d in range(2):
                pl.when(sends(d, s))(lambda d=d, s=s: send(d, s).wait_send())

    def zstep(v, r, s):
        line_step(functools.partial(zsend, v, r), functools.partial(zin, v, r), s)

    def zwstep(s):
        line_step(zwsend, zwin, s)

    def ax(v, u, o):
        cols = pl.ds(pl.multiple_of(fr * tc, tc), tc)
        dst = (fr + o) % n_frame
        rows = pl.ds(u * Lu, Lu)
        return rcopy(
            A.at[v, dst, rows], C.at[v, rows, cols], a_s.at[0], a_r.at[0], {"frame": dst}
        )

    def attx(v):
        return rcopy(att.at[v, :, 1 - core], att2.at[v], at_s.at[v], at_r.at[v], sib)

    wso_x = rcopy(wso_hbm, wso.at[1], so_s.at[0], so_r.at[0], sib)

    ND = n_space * n_frame
    me = fr * n_space + sp

    def ls(o):
        to = (me + o) % ND
        return rcopy(
            LS.at[me], LS.at[me], l_s.at[0], l_r.at[0],
            {"frame": to // n_space, "space": to % n_space},
        )

    def norm_chip(v, c, slot):
        for e in range(2):
            x = norm_mod(G[v, c, e].astype(F32), mod(v, 0), mod(v, 1))
            X[pl.ds(slot * 2 * L + e * L, L)] = x

    def masks():
        nt = tiles_ref.shape[1]
        qt = lax.broadcasted_iota(jnp.int32, (nt, nt), 0)
        kt = lax.broadcasted_iota(jnp.int32, (nt, nt), 1)
        ids = (
            lax.broadcasted_iota(jnp.int32, (span, nt), 0) // TILE
            == lax.broadcasted_iota(jnp.int32, (span, nt), 1)
        ).astype(BF16)
        for v in range(V):
            ok = ((tiles_ref[v] == 1) & (kt < valid_ref[v, 1])) | (qt == kt)
            rows = jnp.dot(ids, ok.astype(BF16), preferred_element_type=F32).astype(BF16)
            full = lax.dot_general(rows, ids, (((1,), (1,)), ((), ())), preferred_element_type=F32)
            smask[v] = jnp.where(full > 0.5, 0.0, -1e30).astype(BF16)

    QB = 256
    XB = X.shape[0]
    pc = XB // (2 * L)

    def spatial_qkv(m):
        def step(j, _):
            qkv[j, pl.ds(pl.multiple_of(m * XB, XB), XB), :] = jnp.dot(
                X[...], wq[j], preferred_element_type=F32
            ).astype(BF16)
            return 0

        lax.fori_loop(0, 3, step, 0)

    def spatial_att(v):
        mt = QB // (2 * L)
        for h in range(sc // HEAD_DIM):
            hs = slice(h * HEAD_DIM, (h + 1) * HEAD_DIM)

            def step(i, _):
                rows = pl.ds(pl.multiple_of(i * QB, QB), QB)
                out = attend(
                    qkv[0, rows, hs], qkv[1, :, hs], qkv[2, :, hs], smask[v, rows, :].astype(F32)
                )
                att[v, pl.ds(i * mt, mt), :, :, hs] = out.reshape(mt, 2, L, HEAD_DIM)
                return 0

            lax.fori_loop(0, span // QB, step, 0)

    CB = 512

    def spatial_out(v):
        def step(i, _):
            cols = pl.ds(pl.multiple_of(i * CB, CB), CB)
            mine = att[v, :, core].reshape(nch * L, sc)
            other = att2[v].reshape(nch * L, sc)
            t = jnp.dot(mine, wso[0, :, cols], preferred_element_type=F32)
            t = t + jnp.dot(other, wso[1, :, cols], preferred_element_type=F32)
            G[v, :, core, :, cols] = t.astype(BF16).reshape(nch, L, CB)
            return 0

        lax.fori_loop(0, D // CB, step, 0)

    def rs_start(v, r):
        for k in range(2):
            for h in range(2):
                for i, j in rs_first(h)[k]:
                    rs(v, r, h, i, j, True).start()

    def rs_relay(v, r):
        for h in range(2):
            for b in range(1, ny if h == 0 else nx):
                if h == 0:
                    srcs, i, j = [(i, b) for i in range(1, nx)], 0, b
                else:
                    srcs, i, j = [(b, j) for j in range(1, ny)], b, 0
                c = chip_to(i, j)
                total = G[v, c, core, piece(r), side(h)].astype(F32)
                for a in srcs:
                    rs(v, r, h, a[0], a[1], True).wait_recv()
                    total = total + R[v, h, at(a[0], a[1]), piece(r)].astype(F32)
                G[v, c, core, piece(r), side(h)] = total.astype(BF16)
                rs(v, r, h, i, j, False).start()

    def finish(v, r):
        rows = piece(r)
        parts = []
        for h in range(2):
            so = G[v, chip, core, rows, side(h)].astype(F32)
            if h == 0:
                order = [(i, 0) for i in range(1, nx)] + [(0, j) for j in range(1, ny)]
            else:
                order = [(0, j) for j in range(1, ny)] + [(i, 0) for i in range(1, nx)]
            for i, j in order:
                rs(v, r, h, i, j, True).wait_recv()
                so = so + R[v, h, at(i, j), rows].astype(F32)
            parts.append(so)
        so = jnp.concatenate(parts, -1)
        x1 = (lat[v, rows].astype(F32) + mod(v, 2) * so).astype(BF16)
        x1_ref[v, rows] = x1
        H[v, fr, rows] = norm_mod(x1.astype(F32), mod(v, 3), mod(v, 4))
        zstep(v, r, 0)

    def temporal(v, u):
        NB = 256
        nn = tc // NB
        tl = n_frame * Lu
        rows = slice(u * Lu, (u + 1) * Lu)

        def step(i, _):
            j, n = i // nn, i % nn
            cols = pl.ds(pl.multiple_of(n * NB, NB), NB)
            x = H[v, :, rows, :].reshape(tl, D)
            tqkv[j, :, cols] = jnp.dot(x, wt[j, :, cols], preferred_element_type=F32).astype(BF16)
            return 0

        lax.fori_loop(0, 3 * nn, step, 0)
        q = lax.broadcasted_iota(jnp.int32, (tl, tl), 0)
        k = lax.broadcasted_iota(jnp.int32, (tl, tl), 1)
        ok = (q % Lu == k % Lu) & ((k // Lu < valid_ref[v, 0]) | (q // Lu == k // Lu))
        bias = jnp.where(ok, 0.0, -1e30)
        for h in range(tc // HEAD_DIM):
            hs = slice(h * HEAD_DIM, (h + 1) * HEAD_DIM)
            out = attend(tqkv[0, :, hs], tqkv[1, :, hs], tqkv[2, :, hs], bias)
            A[v, :, rows, hs] = out.reshape(n_frame, Lu, HEAD_DIM)
        for o in range(1, n_frame):
            ax(v, u, o).start()
        C[v, rows, pl.ds(pl.multiple_of(fr * tc, tc), tc)] = A[v, fr, rows]

    def load_mod(ks):
        for k in ks:
            wm(k).start()

    def take_mod(ks):
        for q in sorted({k % chunks // per for k in ks}):
            n = sum(1 for k in ks if k % chunks // per == q)
            drain(wt.at[q, pl.ds(0, n * FREQ)], wm_sem.at[q])
        for k in ks:
            mod_chunk(k)

    def gather_first(v):
        for h, i, j in FIRST:
            ag_in(v, h, i, j).wait_recv()
            for t in relays_of(h, i, j):
                ag(v, *t).start()
            fw(v, h, i, j).start()

    def gather_second(v):
        for h, i, j in SECOND:
            ag_in(v, h, i, j).wait_recv()
            fw(v, h, i, j).start()

    def gather_third(v):
        for h, i, j in THIRD:
            ag_in(v, h, i, j).wait_recv()
            fw(v, h, i, j).start()

    def own_load(v):
        return pltpu.make_async_copy(lat_hbm.at[v], G.at[v, chip, core], own_sem.at[v])

    def gather_own(v):
        for t in OWN_SENDS:
            ag(v, *t).start()
        for h in range(2):
            fw(v, h, 0, 0).start()

    def gather_end(v):
        n = len(ALL) // 2
        drain(G.at[v, pl.ds(0, n), core], ag_s.at[v])
        drain(G.at[v, :, core], fw_s.at[v])

    def near_qkv(v):
        drain(G.at[v, pl.ds(0, nx), 1 - core], fw_r.at[v, 0])
        for b in range(nx // pc):
            for i in range(pc):
                norm_chip(v, cy * nx + b * pc + i, i)
            if v == 0 and b == 0:
                ld_wq.wait()
            spatial_qkv(cy * (nx // pc) + b)

    def far_qkv(v):
        drain(G.at[v, pl.ds(0, nx * (ny - 1)), 1 - core], fw_r.at[v, 1])
        for j in range(1, ny):
            row = (cy + j) % ny
            for b in range(nx // pc):
                for i in range(pc):
                    norm_chip(v, row * nx + b * pc + i, i)
                spatial_qkv(row * (nx // pc) + b)

    def spatial(v, after_att):
        far_qkv(v)
        spatial_att(v)
        attx(v).start()
        after_att()
        gather_end(v)
        if v == 0:
            ld_wso.wait()
            wso_x.wait_recv()
        attx(v).wait_recv()
        spatial_out(v)

    def weights_own(o, part):
        for t in FIRST if part == 0 else SECOND:
            wg(o, *t).start()
        if part == 0:
            for h in range(2):
                wf(o, h, 0, 0).start()

    def weights_first(o):
        for h, i, j in FIRST:
            wg_in(o, h, i, j).wait_recv()
            for t in relays_of(h, i, j):
                wg(o, *t).start()
            wf(o, h, i, j).start()

    def weights_rest(o):
        for h, i, j in SECOND + THIRD:
            wg_in(o, h, i, j).wait_recv()
            wf(o, h, i, j).start()

    def scatter(v, hooks):
        rs_start(v, 0)
        for r in range(NR):
            rs_relay(v, r)
            if r + 1 < NR:
                rs_start(v, r + 1)
            hooks[r]()
            finish(v, r)

    def late(v, r):
        for s in range(3, n_frame):
            zstep(v, r, s)

    ld_own = [own_load(v) for v in range(V)]
    ld_own[0].start()
    load_mod(range(min(chunks, ncol)))
    ld_own[1].start()
    ld_wq.start()
    ld_own[0].wait()
    pl.semaphore_wait(bar, n_space * n_frame - 1)
    gather_own(0)
    zwstep(0)
    wso_x.start()
    masks()
    gather_first(0)
    ld_own[1].wait()
    gather_own(1)
    ld_wso.start()
    ld_lat.start()
    take_mod(range(min(chunks, ncol)))
    for m in range(1, mod_rounds):
        ks = range(m * chunks, min((m + 1) * chunks, ncol))
        load_mod(ks)
        take_mod(ks)
    ld_wt.start()
    ld_wto.start()
    ld_tgt.start()
    zwstep(1)
    gather_second(0)
    near_qkv(0)
    gather_third(0)
    spatial(0, lambda: zwstep(2))
    ld_lat.wait()

    def end0():
        gather_first(1)
        gather_second(1)
        zstep(0, 0, 2)
        near_qkv(1)
        zstep(0, 1, 1)

    scatter(0, (lambda: None, lambda: zstep(0, 0, 1), end0))
    for s in range(3, n_frame):
        zwstep(s)
    weights_own(1, 0)
    weights_own(1, 1)
    zstep(0, 1, 2)
    gather_third(1)
    spatial(1, lambda: zstep(0, 2, 1))

    def end1():
        weights_first(1)
        for o in range(2, n_frame):
            weights_own(o, 0)
            weights_own(o, 1)
        late(0, 0)
        late(0, 1)
        ld_wt.wait()
        zstep(1, 0, 1)
        temporal(0, 0)

    scatter(1, (lambda: zstep(0, 2, 2), lambda: None, end1))
    zstep(1, 1, 1)
    zstep(1, 0, 2)
    late(0, 2)
    temporal(0, 1)
    zstep(1, 1, 2)
    zstep(1, 2, 1)
    weights_rest(1)
    late(1, 0)
    late(1, 1)
    zstep(1, 2, 2)
    temporal(1, 0)
    for o in range(2, n_frame):
        weights_first(o)
    late(1, 2)
    temporal(1, 1)
    for o in range(2, n_frame):
        weights_rest(o)

    wrows = (n_frame - 1) * 2 * U
    drain(WO.at[pl.ds(0, wrows * nch), pl.ds(0, Dh)], wf_r.at[0])
    drain(C.at[:, :, pl.ds(0, (n_frame - 1) * tc)], a_r.at[0])
    ld_tgt.wait()
    ld_wto.wait()

    def out_step(i, total):
        cols = pl.ds(pl.multiple_of(i * CB, CB), CB)
        a = C[...].reshape(V * L, n_frame * tc)
        acc = jnp.dot(a, WO[:, cols], preferred_element_type=F32)
        part = []
        for v in range(V):
            gate = MOD[5, v : v + 1, cols]
            m = x1_ref[v, :, cols].astype(F32) + gate * acc[v * L : (v + 1) * L]
            m = m.astype(BF16)
            mixed_ref[v, :, cols] = m
            diff = m.astype(F32) - tgt[v, :, cols].astype(F32)
            part.append(jnp.sum(diff * diff, -1, keepdims=True))
        return total + jnp.concatenate(part, 0)

    squares = lax.fori_loop(0, D // CB, out_step, jnp.zeros((V * L, 1), F32)) * (1.0 / D)
    place = sp * L + lax.broadcasted_iota(jnp.int32, (L, 1), 0)
    here = jnp.zeros((1, 1), F32)
    count = jnp.int32(0)
    for v in range(V):
        keep = (place // TILE < valid_ref[v, 1]) & (fr < valid_ref[v, 0])
        here = here + jnp.sum(
            jnp.where(keep, squares[v * L : (v + 1) * L], 0.0), 0, keepdims=True
        )
        count = count + valid_ref[v, 0] * valid_ref[v, 1]
    LS[me] = jnp.broadcast_to(here, (8, 128))
    for o in range(1, ND):
        ls(o).start()
    drain(LS.at[pl.ds(0, ND - 1)], l_r.at[0])
    loss_ref[0, 0] = jnp.sum(jnp.sum(LS[...], 0)[0:1, 0:1]) / (count.astype(F32) * TILE)

    wso_x.wait_send()
    for v in range(V):
        attx(v).wait_send()
        drain(G.at[v, pl.ds(0, nch - 1), core], rs_s.at[v])
        for r in range(NR):
            line_end(functools.partial(zsend, v, r))
    line_end(zwsend)
    drain(C.at[:, :, pl.ds(0, (n_frame - 1) * tc)], a_s.at[0])
    drain(WO.at[pl.ds(0, wrows * (nch - 1)), pl.ds(0, Dh)], wg_s.at[0])
    drain(WO.at[pl.ds(0, wrows * nch), pl.ds(0, Dh)], wf_s.at[0])
    drain(LS.at[pl.ds(0, ND - 1)], l_s.at[0])


def run_kernel(timesteps, valid, tile_mask, latents, w_mod, w_sqkv, w_sout, w_tqkv, w_tout, target):
    V, L, D = latents.shape
    n_space = lax.axis_size("space")
    n_frame = lax.axis_size("frame")
    nch = n_space // 2
    ny = 2 if nch % 2 == 0 else 1
    nx = nch // ny
    NR = len(ROUNDS)
    sc, tc = w_sqkv.shape[2], w_tqkv.shape[2]
    span = n_space * L
    tl = n_frame * L // UNITS
    far = nx * ny - 1
    n1 = n_frame - 1
    dma = pltpu.SemaphoreType.DMA
    vm = pl.BlockSpec(memory_space=pltpu.VMEM)
    sm = pl.BlockSpec(memory_space=pltpu.SMEM)
    hbm = pl.BlockSpec(memory_space=pl.ANY)
    return pl.pallas_call(
        functools.partial(kernel, n_space, n_frame, nx, ny),
        out_shape=(
            jax.ShapeDtypeStruct((V, L, D), BF16),
            jax.ShapeDtypeStruct((1, 1), F32),
        ),
        in_specs=[sm, sm, vm] + [hbm] * 7,
        out_specs=(vm, sm),
        scratch_shapes=[
            pltpu.VMEM((V, L, D), BF16),
            pltpu.VMEM((V, L, D), BF16),
            pltpu.VMEM((6, 8, D), F32),
            pltpu.VMEM((V, nch, 2, L, D), BF16),
            pltpu.VMEM((256, D), BF16),
            pltpu.VMEM((V, 2, far, L, D // 2), BF16),
            pltpu.VMEM((V, n_frame, L, D), BF16),
            pltpu.VMEM((V, L, n_frame * tc), BF16),
            pltpu.VMEM((V, L, D), BF16),
            pltpu.VMEM((n_frame * w_tout.shape[0], D), BF16),
            pltpu.VMEM(w_sqkv.shape, BF16),
            pltpu.VMEM((2,) + w_sout.shape, BF16),
            pltpu.VMEM(w_tqkv.shape, BF16),
            pltpu.VMEM((3, span, sc), BF16),
            pltpu.VMEM((V, nch, 2, L, sc), BF16),
            pltpu.VMEM((V, nch, L, sc), BF16),
            pltpu.VMEM((3, tl, tc), BF16),
            pltpu.VMEM((V, n_frame, L, tc), BF16),
            pltpu.VMEM((V, span, span), BF16),
            pltpu.VMEM((n_space * n_frame, 8, 128), F32),
            dma((V,)), dma((V, 2, far)), dma((V,)), dma((V, 2)),
            dma((V,)), dma((V, NR, 2, far)),
            dma((V, NR, 2, n1)), dma((V, NR, 2, n1)),
            dma((1,)), dma((1,)),
            dma((2, n1)), dma((2, n1)),
            dma((1,)), dma((n1, 2, far)), dma((1,)), dma((1,)),
            dma((V,)), dma((V,)), dma((1,)), dma((1,)),
            dma((1,)), dma((1,)),
            dma((6,)), dma((V,)), dma((3,)),
        ],
        compiler_params=pltpu.CompilerParams(
            collective_id=0, has_side_effects=True, vmem_limit_bytes=61 * 1024 * 1024
        ),
        cost_estimate=pl.CostEstimate(
            flops=14_000_000_000, bytes_accessed=35_000_000, transcendentals=3_000_000
        ),
        name="block",
    )(timesteps, valid, tile_mask, latents, w_mod, w_sqkv, w_sout, w_tqkv, w_tout, target)


def shards(latents, target, timesteps, valid, tile_mask, w_mod, w_sqkv, w_sout, w_tqkv, w_tout):
    videos, frames_dev, span_dev, width = latents.shape
    shape = (videos, span_dev, width)
    mixed, loss = run_kernel(
        timesteps, valid, tile_mask, latents.reshape(shape), w_mod,
        w_sqkv, w_sout, w_tqkv, w_tout, target.reshape(shape),
    )
    return (mixed.reshape(latents.shape), loss.reshape(()))


def solution(mesh):
    return jax.shard_map(
        shards,
        mesh=mesh,
        in_specs=(
            P(None, "frame", "space", None),
            P(None, "frame", "space", None),
            P(),
            P(),
            P(),
            P(),
            P(None, None, "space"),
            P("space", None),
            P(None, None, "frame"),
            P("frame", None),
        ),
        out_specs=(P(None, "frame", "space", None), P()),
        check_vma=False,
    )
```

```python
import functools
import math

import jax
import jax.numpy as jnp
from jax import lax
from jax.experimental import pallas as pl
from jax.experimental.pallas import tpu as pltpu
from jax.sharding import PartitionSpec as P

HEAD_DIM = 128
FREQ = 256
TILE = 32
ROUNDS = ((0, 4), (4, 4), (8, 8))
UNITS = 2
MESH = pl.DeviceIdType.MESH
F32 = jnp.float32
BF16 = jnp.bfloat16


def norm_mod(values, shift, scale):
    mean = jnp.mean(values, -1, keepdims=True)
    centred = values - mean
    var = jnp.mean(centred * centred, -1, keepdims=True)
    return (centred * lax.rsqrt(var + 1e-06) * (1.0 + scale) + shift).astype(BF16)


def attend(query, keys, values, bias):
    scores = lax.dot_general(query, keys, (((1,), (1,)), ((), ())), preferred_element_type=F32)
    scores = scores * (math.log2(math.e) / math.sqrt(HEAD_DIM)) + bias
    top = jnp.max(scores, -1, keepdims=True)
    weights = jnp.exp2(scores - top)
    total = jnp.sum(weights, -1, keepdims=True)
    out = jnp.dot(weights.astype(BF16), values, preferred_element_type=F32)
    return (out * (1.0 / total)).astype(BF16)


def kernel(
    n_space, n_frame, nx, ny,
    ts_ref, valid_ref, tiles_ref, lat_hbm, wmod_hbm, wq_hbm, wso_hbm, wt_hbm, wto_hbm, tgt_hbm,
    mixed_ref, loss_ref,
    lat, tgt, MOD, G, X, R, H, C, x1_ref, WO, wq, wso, wt, qkv, att, att2, tqkv, A, smask, LS,
    ag_s, ag_r, fw_s, fw_r, rs_s, rs_r, z_s, z_r, a_s, a_r, zw_s, zw_r, wg_s, wg_r, wf_s, wf_r,
    at_s, at_r, so_s, so_r, l_s, l_r, ld_sem, own_sem, wm_sem, put_sem, mixb,
):
    V, L, D = lat.shape
    nch = n_space // 2
    span = n_space * L
    NR = len(ROUNDS)
    NU = UNITS
    Lu, Lh, Dh = L // NU, L // 2, D // 2
    sp = lax.axis_index("space")
    fr = lax.axis_index("frame")
    core = sp % 2
    chip = sp // 2
    cx, cy = chip % nx, chip // nx
    FR = wto_hbm.shape[0]
    U = FR // n_space
    sc, tc = wq.shape[2], wt.shape[2]
    sib = {"space": chip * 2 + (1 - core)}

    def chip_at(i, j):
        return ((cy + ny - j) % ny) * nx + (cx + nx - i) % nx

    def chip_to(i, j):
        return ((cy + j) % ny) * nx + (cx + i) % nx

    def at(i, j):
        return j * nx + i - 1

    def drain(ref, sem):
        pltpu.make_async_copy(ref, ref, sem).wait()

    def rcopy(src, dst, s, r, dev):
        return pltpu.make_async_remote_copy(
            src_ref=src, dst_ref=dst, send_sem=s, recv_sem=r, device_id=dev, device_id_type=MESH
        )

    def dev_to(i, j):
        return {"space": chip_to(i, j) * 2 + core}

    chunks = wt.shape[0] * (wt.shape[1] // FREQ)
    ncol = wmod_hbm.shape[1] // tc
    mod_rounds = (ncol + chunks - 1) // chunks
    per = wt.shape[1] // FREQ

    def wm(k):
        q = k % chunks
        return pltpu.make_async_copy(
            wmod_hbm.at[:, pl.ds(k * tc, tc)],
            wt.at[q // per, pl.ds((q % per) * FREQ, FREQ)],
            wm_sem.at[q // per],
        )

    ld_lat = pltpu.make_async_copy(lat_hbm, lat, ld_sem.at[0])
    ld_wq = pltpu.make_async_copy(wq_hbm, wq, ld_sem.at[1])
    ld_wso = pltpu.make_async_copy(wso_hbm, wso.at[0], ld_sem.at[2])
    ld_wt = pltpu.make_async_copy(wt_hbm, wt, ld_sem.at[3])
    ld_wto = pltpu.make_async_copy(
        wto_hbm, WO.at[pl.ds(pl.multiple_of(fr * FR, FR), FR)], ld_sem.at[4]
    )
    ld_tgt = pltpu.make_async_copy(tgt_hbm, tgt, ld_sem.at[5])

    bar = pltpu.get_barrier_semaphore()
    for o in range(1, n_space * n_frame):
        to = (fr * n_space + sp + o) % (n_space * n_frame)
        pl.semaphore_signal(
            bar, inc=1, device_id={"frame": to // n_space, "space": to % n_space}, device_id_type=MESH
        )

    half = FREQ // 2
    lane = lax.broadcasted_iota(jnp.int32, (8, half), 1).astype(F32)
    rows8 = lax.broadcasted_iota(jnp.int32, (8, half), 0)
    steps = jnp.zeros((8, half), F32)
    for v in range(V):
        steps = jnp.where(rows8 == v, ts_ref[v].astype(F32), steps)
    angles = steps * jnp.exp(-math.log(10000.0) * lane / half)
    embed = jnp.concatenate([jnp.cos(angles), jnp.sin(angles)], -1).astype(BF16)

    def mod_chunk(k):
        q = k % chunks
        w = wt[q // per, pl.ds((q % per) * FREQ, FREQ), :]
        sec, col = (k * tc) // D, (k * tc) % D
        MOD[sec, :, col : col + tc] = jnp.dot(embed, w, preferred_element_type=F32)

    def mod(v, i):
        return MOD[i, v : v + 1, :]

    def send2(blk, ss, rs, h, i, j):
        if h == 0:
            src = blk(chip, 0) if j == 0 else blk(chip_at(i, 0), 0)
            dev = dev_to(i, 0) if j == 0 else dev_to(0, j)
        else:
            src = blk(chip, 1) if i == 0 else blk(chip_at(0, j), 1)
            dev = dev_to(0, j) if i == 0 else dev_to(i, 0)
        return rcopy(src, src, ss, rs, dev)

    def recv2(blk, ss, rs, h, i, j):
        slot = blk(chip_at(i, j), h)
        return rcopy(slot, slot, ss, rs, sib)

    OFFS = [(i, j) for j in range(ny) for i in range(nx)]
    FIRST = [(0, i, 0) for i in range(1, nx)] + [(1, 0, j) for j in range(1, ny)]

    def relays_of(h, i, j):
        if h == 0:
            return [(0, i, jj) for jj in range(1, ny)]
        return [(1, ii, j) for ii in range(1, nx)]

    SECOND = [(0, 0, j) for j in range(1, ny)] + [(1, i, 0) for i in range(1, nx)]
    OWN_SENDS = FIRST + SECOND
    THIRD = [(h, i, j) for h in range(2) for j in range(1, ny) for i in range(1, nx)]
    ALL = [(h, i, j) for h in range(2) for (i, j) in OFFS if (i, j) != (0, 0)]

    def tok(v):
        return lambda c, h: G.at[v, c, core, pl.ds(h * Lh, Lh)]

    def ag(v, h, i, j):
        return send2(tok(v), ag_s.at[v], ag_r.at[v, h, at(i, j)], h, i, j)

    def ag_in(v, h, i, j):
        return recv2(tok(v), ag_s.at[v], ag_r.at[v, h, at(i, j)], h, i, j)

    def fw(v, h, i, j):
        slot = G.at[v, chip_at(i, j), core, pl.ds(h * Lh, Lh)]
        return rcopy(slot, slot, fw_s.at[v], fw_r.at[v, min(j, 1)], sib)

    def unit(f, s, h):
        row = pl.multiple_of(f * FR + s * U, U)
        return WO.at[pl.ds(row, U), pl.ds(h * (D // 2), D // 2)]

    def wrow(o):
        return lambda c, h: unit((fr + o) % n_frame, c * 2 + core, h)

    def wg(o, h, i, j):
        return send2(wrow(o), wg_s.at[0], wg_r.at[o - 1, h, at(i, j)], h, i, j)

    def wg_in(o, h, i, j):
        return recv2(wrow(o), wg_s.at[0], wg_r.at[o - 1, h, at(i, j)], h, i, j)

    def wf(o, h, i, j):
        slot = unit((fr + o) % n_frame, chip_at(i, j) * 2 + core, h)
        return rcopy(slot, slot, wf_s.at[0], wf_r.at[0], sib)

    def piece(r):
        a, n = ROUNDS[r]
        return pl.ds(a * L // 16, n * L // 16)

    def side(h):
        return pl.ds(h * Dh, Dh)

    def rs(v, r, h, i, j, first):
        src = G.at[v, chip_to(i, j), core, piece(r), side(h)]
        if h == 0:
            dev = dev_to(i, 0) if first else dev_to(0, j)
        else:
            dev = dev_to(0, j) if first else dev_to(i, 0)
        return rcopy(
            src, R.at[v, h, at(i, j), piece(r)], rs_s.at[v], rs_r.at[v, r, h, at(i, j)], dev
        )

    def rs_first(h):
        if h == 0:
            far = [(i, j) for i in range(1, nx) for j in range(1, ny)]
            near = [(i, 0) for i in range(1, nx)]
        else:
            far = [(i, j) for j in range(1, ny) for i in range(1, nx)]
            near = [(0, j) for j in range(1, ny)]
        return far, near

    def hblk(v, r, f):
        return H.at[v, f, piece(r)]

    def zsend(v, r, d, s):
        f = fr - s if d == 0 else fr + s
        to = fr + 1 if d == 0 else fr - 1
        blk = hblk(v, r, f)
        return rcopy(blk, blk, z_s.at[v, r, d, s], z_r.at[v, r, d, s], {"frame": to})

    def zin(v, r, d, s):
        f = fr - s if d == 0 else fr + s
        blk = hblk(v, r, f)
        return rcopy(blk, blk, z_s.at[v, r, d, s - 1], z_r.at[v, r, d, s - 1], sib)

    def wunit(f):
        return WO.at[pl.ds(pl.multiple_of(f * FR + sp * U, U), U)]

    def zwsend(d, s):
        f = fr - s if d == 0 else fr + s
        to = fr + 1 if d == 0 else fr - 1
        src = wto_hbm.at[pl.ds(pl.multiple_of(sp * U, U), U)] if s == 0 else wunit(f)
        return rcopy(src, wunit(f), zw_s.at[d, s], zw_r.at[d, s], {"frame": to})

    def zwin(d, s):
        f = fr - s if d == 0 else fr + s
        return rcopy(wunit(f), wunit(f), zw_s.at[d, s - 1], zw_r.at[d, s - 1], sib)

    def has(d, s):
        return fr >= s if d == 0 else fr + s < n_frame

    def sends(d, s):
        if d == 0:
            return (fr >= s) & (fr + 1 < n_frame)
        return (fr + s < n_frame) & (fr >= 1)

    def line_step(send, arrive, s):
        for d in range(2):
            if s > 0:
                pl.when(has(d, s))(lambda d=d: arrive(d, s).wait_recv())
            if s < n_frame - 1:
                pl.when(sends(d, s))(lambda d=d: send(d, s).start())

    def line_end(send):
        for s in range(n_frame - 1):
            for d in range(2):
                pl.when(sends(d, s))(lambda d=d, s=s: send(d, s).wait_send())

    def zstep(v, r, s):
        line_step(functools.partial(zsend, v, r), functools.partial(zin, v, r), s)

    def zwstep(s):
        line_step(zwsend, zwin, s)

    def ax(v, u, o):
        cols = pl.ds(pl.multiple_of(fr * tc, tc), tc)
        dst = (fr + o) % n_frame
        rows = pl.ds(u * Lu, Lu)
        return rcopy(
            A.at[v, dst, rows], C.at[v, rows, cols], a_s.at[0], a_r.at[0], {"frame": dst}
        )

    def attx(v):
        return rcopy(att.at[v, :, 1 - core], att2.at[v], at_s.at[v], at_r.at[v], sib)

    wso_x = rcopy(wso_hbm, wso.at[1], so_s.at[0], so_r.at[0], sib)

    ND = n_space * n_frame
    me = fr * n_space + sp

    def ls(o):
        to = (me + o) % ND
        return rcopy(
            LS.at[me], LS.at[me], l_s.at[0], l_r.at[0],
            {"frame": to // n_space, "space": to % n_space},
        )

    def norm_chip(v, c, slot):
        for e in range(2):
            x = norm_mod(G[v, c, e].astype(F32), mod(v, 0), mod(v, 1))
            X[pl.ds(slot * 2 * L + e * L, L)] = x

    def masks():
        nt = tiles_ref.shape[1]
        qt = lax.broadcasted_iota(jnp.int32, (nt, nt), 0)
        kt = lax.broadcasted_iota(jnp.int32, (nt, nt), 1)
        ids = (
            lax.broadcasted_iota(jnp.int32, (span, nt), 0) // TILE
            == lax.broadcasted_iota(jnp.int32, (span, nt), 1)
        ).astype(BF16)
        for v in range(V):
            ok = ((tiles_ref[v] == 1) & (kt < valid_ref[v, 1])) | (qt == kt)
            rows = jnp.dot(ids, ok.astype(BF16), preferred_element_type=F32).astype(BF16)
            full = lax.dot_general(rows, ids, (((1,), (1,)), ((), ())), preferred_element_type=F32)
            smask[v] = jnp.where(full > 0.5, 0.0, -1e30).astype(BF16)

    QB = 256
    XB = X.shape[0]
    pc = XB // (2 * L)

    def spatial_qkv(m):
        def step(j, _):
            qkv[j, pl.ds(pl.multiple_of(m * XB, XB), XB), :] = jnp.dot(
                X[...], wq[j], preferred_element_type=F32
            ).astype(BF16)
            return 0

        lax.fori_loop(0, 3, step, 0)

    def spatial_att(v):
        mt = QB // (2 * L)

        def step(i, _):
            rows = pl.ds(pl.multiple_of(i * QB, QB), QB)
            bias = smask[v, rows, :].astype(F32)
            for h in range(sc // HEAD_DIM):
                hs = slice(h * HEAD_DIM, (h + 1) * HEAD_DIM)
                out = attend(qkv[0, rows, hs], qkv[1, :, hs], qkv[2, :, hs], bias)
                att[v, pl.ds(i * mt, mt), :, :, hs] = out.reshape(mt, 2, L, HEAD_DIM)
            return 0

        lax.fori_loop(0, span // QB, step, 0)

    CB = 512

    def spatial_out(v):
        def step(i, _):
            cols = pl.ds(pl.multiple_of(i * CB, CB), CB)
            mine = att[v, :, core].reshape(nch * L, sc)
            other = att2[v].reshape(nch * L, sc)
            t = jnp.dot(mine, wso[0, :, cols], preferred_element_type=F32)
            t = t + jnp.dot(other, wso[1, :, cols], preferred_element_type=F32)
            G[v, :, core, :, cols] = t.astype(BF16).reshape(nch, L, CB)
            return 0

        lax.fori_loop(0, D // CB, step, 0)

    def rs_start(v, r):
        for k in range(2):
            for h in range(2):
                for i, j in rs_first(h)[k]:
                    rs(v, r, h, i, j, True).start()

    def rs_relay(v, r):
        for h in range(2):
            for b in range(1, ny if h == 0 else nx):
                if h == 0:
                    srcs, i, j = [(i, b) for i in range(1, nx)], 0, b
                else:
                    srcs, i, j = [(b, j) for j in range(1, ny)], b, 0
                c = chip_to(i, j)
                total = G[v, c, core, piece(r), side(h)].astype(F32)
                for a in srcs:
                    rs(v, r, h, a[0], a[1], True).wait_recv()
                    total = total + R[v, h, at(a[0], a[1]), piece(r)].astype(F32)
                G[v, c, core, piece(r), side(h)] = total.astype(BF16)
                rs(v, r, h, i, j, False).start()

    def finish(v, r):
        rows = piece(r)
        parts = []
        for h in range(2):
            so = G[v, chip, core, rows, side(h)].astype(F32)
            if h == 0:
                order = [(i, 0) for i in range(1, nx)] + [(0, j) for j in range(1, ny)]
            else:
                order = [(0, j) for j in range(1, ny)] + [(i, 0) for i in range(1, nx)]
            for i, j in order:
                rs(v, r, h, i, j, True).wait_recv()
                so = so + R[v, h, at(i, j), rows].astype(F32)
            parts.append(so)
        so = jnp.concatenate(parts, -1)
        x1 = (lat[v, rows].astype(F32) + mod(v, 2) * so).astype(BF16)
        x1_ref[v, rows] = x1
        H[v, fr, rows] = norm_mod(x1.astype(F32), mod(v, 3), mod(v, 4))
        zstep(v, r, 0)

    def temporal(v, u):
        NB = 256
        nn = tc // NB
        tl = n_frame * Lu
        rows = slice(u * Lu, (u + 1) * Lu)

        def step(i, _):
            j, n = i // nn, i % nn
            cols = pl.ds(pl.multiple_of(n * NB, NB), NB)
            x = H[v, :, rows, :].reshape(tl, D)
            tqkv[j, :, cols] = jnp.dot(x, wt[j, :, cols], preferred_element_type=F32).astype(BF16)
            return 0

        lax.fori_loop(0, 3 * nn, step, 0)
        q = lax.broadcasted_iota(jnp.int32, (tl, tl), 0)
        k = lax.broadcasted_iota(jnp.int32, (tl, tl), 1)
        ok = (q % Lu == k % Lu) & ((k // Lu < valid_ref[v, 0]) | (q // Lu == k // Lu))
        bias = jnp.where(ok, 0.0, -1e30)
        for h in range(tc // HEAD_DIM):
            hs = slice(h * HEAD_DIM, (h + 1) * HEAD_DIM)
            out = attend(tqkv[0, :, hs], tqkv[1, :, hs], tqkv[2, :, hs], bias)
            A[v, :, rows, hs] = out.reshape(n_frame, Lu, HEAD_DIM)
        for o in range(1, n_frame):
            ax(v, u, o).start()
        C[v, rows, pl.ds(pl.multiple_of(fr * tc, tc), tc)] = A[v, fr, rows]

    def load_mod(ks):
        for k in ks:
            wm(k).start()

    def take_mod(ks):
        for q in sorted({k % chunks // per for k in ks}):
            n = sum(1 for k in ks if k % chunks // per == q)
            drain(wt.at[q, pl.ds(0, n * FREQ)], wm_sem.at[q])
        for k in ks:
            mod_chunk(k)

    def gather_first(v):
        for h, i, j in FIRST:
            ag_in(v, h, i, j).wait_recv()
            for t in relays_of(h, i, j):
                ag(v, *t).start()
            fw(v, h, i, j).start()

    def gather_second(v):
        for h, i, j in SECOND:
            ag_in(v, h, i, j).wait_recv()
            fw(v, h, i, j).start()

    def gather_third(v):
        for h, i, j in THIRD:
            ag_in(v, h, i, j).wait_recv()
            fw(v, h, i, j).start()

    def own_load(v):
        return pltpu.make_async_copy(lat_hbm.at[v], G.at[v, chip, core], own_sem.at[v])

    def gather_own(v):
        for t in OWN_SENDS:
            ag(v, *t).start()
        for h in range(2):
            fw(v, h, 0, 0).start()

    def gather_end(v):
        n = len(ALL) // 2
        drain(G.at[v, pl.ds(0, n), core], ag_s.at[v])
        drain(G.at[v, :, core], fw_s.at[v])

    def near_qkv(v):
        drain(G.at[v, pl.ds(0, nx), 1 - core], fw_r.at[v, 0])
        for b in range(nx // pc):
            for i in range(pc):
                norm_chip(v, cy * nx + b * pc + i, i)
            if v == 0 and b == 0:
                ld_wq.wait()
            spatial_qkv(cy * (nx // pc) + b)

    def far_qkv(v):
        drain(G.at[v, pl.ds(0, nx * (ny - 1)), 1 - core], fw_r.at[v, 1])
        for j in range(1, ny):
            row = (cy + j) % ny
            for b in range(nx // pc):
                for i in range(pc):
                    norm_chip(v, row * nx + b * pc + i, i)
                spatial_qkv(row * (nx // pc) + b)

    def attention(v):
        spatial_att(v)
        attx(v).start()

    def project(v):
        gather_end(v)
        if v == 0:
            ld_wso.wait()
            wso_x.wait_recv()
        attx(v).wait_recv()
        spatial_out(v)

    def weights_own(o, part):
        for t in FIRST if part == 0 else SECOND:
            wg(o, *t).start()
        if part == 0:
            for h in range(2):
                wf(o, h, 0, 0).start()

    def weights_first(o):
        for h, i, j in FIRST:
            wg_in(o, h, i, j).wait_recv()
            for t in relays_of(h, i, j):
                wg(o, *t).start()
            wf(o, h, i, j).start()

    def weights_rest(o):
        for h, i, j in SECOND + THIRD:
            wg_in(o, h, i, j).wait_recv()
            wf(o, h, i, j).start()

    def late(v, r):
        for s in range(3, n_frame):
            zstep(v, r, s)

    ld_own = [own_load(v) for v in range(V)]
    ld_own[0].start()
    load_mod(range(min(chunks, ncol)))
    ld_own[1].start()
    ld_wq.start()
    ld_own[0].wait()
    pl.semaphore_wait(bar, n_space * n_frame - 1)
    gather_own(0)
    zwstep(0)
    wso_x.start()
    masks()
    gather_first(0)
    ld_own[1].wait()
    gather_own(1)
    ld_wso.start()
    ld_lat.start()
    take_mod(range(min(chunks, ncol)))
    for m in range(1, mod_rounds):
        ks = range(m * chunks, min((m + 1) * chunks, ncol))
        load_mod(ks)
        take_mod(ks)
    ld_wt.start()
    ld_wto.start()
    ld_tgt.start()
    zwstep(1)
    gather_second(0)
    near_qkv(0)
    gather_third(0)
    far_qkv(0)
    gather_first(1)
    attention(0)
    zwstep(2)
    project(0)
    rs_start(0, 0)
    rs_start(0, 1)
    ld_lat.wait()
    gather_second(1)
    near_qkv(1)
    rs_relay(0, 0)
    rs_relay(0, 1)
    rs_start(0, 2)
    gather_third(1)
    far_qkv(1)
    finish(0, 0)
    finish(0, 1)
    rs_relay(0, 2)
    attention(1)
    zstep(0, 0, 1)
    project(1)
    rs_start(1, 0)
    rs_start(1, 1)
    finish(0, 2)
    zstep(0, 1, 1)
    zstep(0, 0, 2)
    zstep(0, 1, 2)
    rs_relay(1, 0)
    rs_relay(1, 1)
    rs_start(1, 2)
    for s in range(3, n_frame):
        zwstep(s)
    finish(1, 0)
    finish(1, 1)
    rs_relay(1, 2)
    for o in (1, 2):
        weights_own(o, 0)
        weights_own(o, 1)
    zstep(0, 2, 1)
    zstep(0, 2, 2)
    finish(1, 2)
    zstep(1, 0, 1)
    zstep(1, 1, 1)
    late(0, 0)
    late(0, 1)
    ld_wt.wait()
    temporal(0, 0)
    zstep(1, 2, 1)
    zstep(1, 0, 2)
    zstep(1, 1, 2)
    weights_first(1)
    for o in range(3, n_frame):
        weights_own(o, 0)
        weights_own(o, 1)
    late(0, 2)
    temporal(0, 1)
    zstep(1, 2, 2)
    weights_rest(1)
    weights_first(2)
    late(1, 0)
    late(1, 1)
    temporal(1, 0)
    for o in range(3, n_frame):
        weights_first(o)
    late(1, 2)
    temporal(1, 1)
    for o in range(2, n_frame):
        weights_rest(o)

    wrows = (n_frame - 1) * 2 * U
    drain(WO.at[pl.ds(0, wrows * nch), pl.ds(0, Dh)], wf_r.at[0])
    drain(C.at[:, :, pl.ds(0, (n_frame - 1) * tc)], a_r.at[0])
    ld_tgt.wait()
    ld_wto.wait()

    def out_step(i, total):
        cols = pl.ds(pl.multiple_of(i * CB, CB), CB)
        a = C[...].reshape(V * L, n_frame * tc)
        acc = jnp.dot(a, WO[:, cols], preferred_element_type=F32)
        part = []
        for v in range(V):
            gate = MOD[5, v : v + 1, cols]
            m = x1_ref[v, :, cols].astype(F32) + gate * acc[v * L : (v + 1) * L]
            m = m.astype(BF16)
            mixb[v, :, cols] = m
            diff = m.astype(F32) - tgt[v, :, cols].astype(F32)
            part.append(jnp.sum(diff * diff, -1, keepdims=True))
        return total + jnp.concatenate(part, 0)

    squares = lax.fori_loop(0, D // CB, out_step, jnp.zeros((V * L, 1), F32)) * (1.0 / D)
    place = sp * L + lax.broadcasted_iota(jnp.int32, (L, 1), 0)
    here = jnp.zeros((1, 1), F32)
    count = jnp.int32(0)
    for v in range(V):
        keep = (place // TILE < valid_ref[v, 1]) & (fr < valid_ref[v, 0])
        here = here + jnp.sum(
            jnp.where(keep, squares[v * L : (v + 1) * L], 0.0), 0, keepdims=True
        )
        count = count + valid_ref[v, 0] * valid_ref[v, 1]
    put = pltpu.make_async_copy(mixb, mixed_ref, put_sem.at[0])
    put.start()
    LS[me] = jnp.broadcast_to(here, (8, 128))
    for o in range(1, ND):
        ls(o).start()
    drain(LS.at[pl.ds(0, ND - 1)], l_r.at[0])
    loss_ref[0, 0] = jnp.sum(jnp.sum(LS[...], 0)[0:1, 0:1]) / (count.astype(F32) * TILE)

    put.wait()
    wso_x.wait_send()
    for v in range(V):
        attx(v).wait_send()
        drain(G.at[v, pl.ds(0, nch - 1), core], rs_s.at[v])
        for r in range(NR):
            line_end(functools.partial(zsend, v, r))
    line_end(zwsend)
    drain(C.at[:, :, pl.ds(0, (n_frame - 1) * tc)], a_s.at[0])
    drain(WO.at[pl.ds(0, wrows * (nch - 1)), pl.ds(0, Dh)], wg_s.at[0])
    drain(WO.at[pl.ds(0, wrows * nch), pl.ds(0, Dh)], wf_s.at[0])
    drain(LS.at[pl.ds(0, ND - 1)], l_s.at[0])


def run_kernel(timesteps, valid, tile_mask, latents, w_mod, w_sqkv, w_sout, w_tqkv, w_tout, target):
    V, L, D = latents.shape
    n_space = lax.axis_size("space")
    n_frame = lax.axis_size("frame")
    nch = n_space // 2
    ny = 2 if nch % 2 == 0 else 1
    nx = nch // ny
    NR = len(ROUNDS)
    sc, tc = w_sqkv.shape[2], w_tqkv.shape[2]
    span = n_space * L
    tl = n_frame * L // UNITS
    far = nx * ny - 1
    n1 = n_frame - 1
    dma = pltpu.SemaphoreType.DMA
    vm = pl.BlockSpec(memory_space=pltpu.VMEM)
    sm = pl.BlockSpec(memory_space=pltpu.SMEM)
    hbm = pl.BlockSpec(memory_space=pl.ANY)
    return pl.pallas_call(
        functools.partial(kernel, n_space, n_frame, nx, ny),
        out_shape=(
            jax.ShapeDtypeStruct((V, L, D), BF16),
            jax.ShapeDtypeStruct((1, 1), F32),
        ),
        in_specs=[sm, sm, vm] + [hbm] * 7,
        out_specs=(hbm, sm),
        scratch_shapes=[
            pltpu.VMEM((V, L, D), BF16),
            pltpu.VMEM((V, L, D), BF16),
            pltpu.VMEM((6, 8, D), F32),
            pltpu.VMEM((V, nch, 2, L, D), BF16),
            pltpu.VMEM((256, D), BF16),
            pltpu.VMEM((V, 2, far, L, D // 2), BF16),
            pltpu.VMEM((V, n_frame, L, D), BF16),
            pltpu.VMEM((V, L, n_frame * tc), BF16),
            pltpu.VMEM((V, L, D), BF16),
            pltpu.VMEM((n_frame * w_tout.shape[0], D), BF16),
            pltpu.VMEM(w_sqkv.shape, BF16),
            pltpu.VMEM((2,) + w_sout.shape, BF16),
            pltpu.VMEM(w_tqkv.shape, BF16),
            pltpu.VMEM((3, span, sc), BF16),
            pltpu.VMEM((V, nch, 2, L, sc), BF16),
            pltpu.VMEM((V, nch, L, sc), BF16),
            pltpu.VMEM((3, tl, tc), BF16),
            pltpu.VMEM((V, n_frame, L, tc), BF16),
            pltpu.VMEM((V, span, span), BF16),
            pltpu.VMEM((n_space * n_frame, 8, 128), F32),
            dma((V,)), dma((V, 2, far)), dma((V,)), dma((V, 2)),
            dma((V,)), dma((V, NR, 2, far)),
            dma((V, NR, 2, n1)), dma((V, NR, 2, n1)),
            dma((1,)), dma((1,)),
            dma((2, n1)), dma((2, n1)),
            dma((1,)), dma((n1, 2, far)), dma((1,)), dma((1,)),
            dma((V,)), dma((V,)), dma((1,)), dma((1,)),
            dma((1,)), dma((1,)),
            dma((6,)), dma((V,)), dma((3,)), dma((1,)),
            pltpu.VMEM((V, L, D), BF16),
        ],
        compiler_params=pltpu.CompilerParams(
            collective_id=0, has_side_effects=True, vmem_limit_bytes=61 * 1024 * 1024
        ),
        cost_estimate=pl.CostEstimate(
            flops=14_000_000_000, bytes_accessed=35_000_000, transcendentals=3_000_000
        ),
        name="block",
    )(timesteps, valid, tile_mask, latents, w_mod, w_sqkv, w_sout, w_tqkv, w_tout, target)


def shards(latents, target, timesteps, valid, tile_mask, w_mod, w_sqkv, w_sout, w_tqkv, w_tout):
    videos, frames_dev, span_dev, width = latents.shape
    shape = (videos, span_dev, width)
    mixed, loss = run_kernel(
        timesteps, valid, tile_mask, latents.reshape(shape), w_mod,
        w_sqkv, w_sout, w_tqkv, w_tout, target.reshape(shape),
    )
    return (mixed.reshape(latents.shape), loss.reshape(()))


def solution(mesh):
    return jax.shard_map(
        shards,
        mesh=mesh,
        in_specs=(
            P(None, "frame", "space", None),
            P(None, "frame", "space", None),
            P(),
            P(),
            P(),
            P(),
            P(None, None, "space"),
            P("space", None),
            P(None, None, "frame"),
            P("frame", None),
        ),
        out_specs=(P(None, "frame", "space", None), P()),
        check_vma=False,
    )
```

```python
import functools
import math

import jax
import jax.numpy as jnp
from jax import lax
from jax.experimental import pallas as pl
from jax.experimental.pallas import tpu as pltpu
from jax.sharding import PartitionSpec as P

HEAD_DIM = 128
FREQ = 256
TILE = 32
ROUNDS = ((0, 4), (4, 4), (8, 8))
UNITS = 2
MESH = pl.DeviceIdType.MESH
F32 = jnp.float32
BF16 = jnp.bfloat16


def norm_mod(values, shift, scale):
    mean = jnp.mean(values, -1, keepdims=True)
    centred = values - mean
    var = jnp.mean(centred * centred, -1, keepdims=True)
    return (centred * lax.rsqrt(var + 1e-06) * (1.0 + scale) + shift).astype(BF16)


def attend(query, keys, values, bias):
    scores = lax.dot_general(query, keys, (((1,), (1,)), ((), ())), preferred_element_type=F32)
    scores = scores * (math.log2(math.e) / math.sqrt(HEAD_DIM)) + bias
    top = jnp.max(scores, -1, keepdims=True)
    weights = jnp.exp2(scores - top)
    total = jnp.sum(weights, -1, keepdims=True)
    out = jnp.dot(weights.astype(BF16), values, preferred_element_type=F32)
    return (out * (1.0 / total)).astype(BF16)


def kernel(
    n_space, n_frame, nx, ny,
    ts_ref, valid_ref, tiles_ref, lat_hbm, wmod_hbm, wq_hbm, wso_hbm, wt_hbm, wto_hbm, tgt_hbm,
    mixed_ref, loss_ref,
    lat, tgt, MOD, G, X, R, H, C, x1_ref, WO, wq, wso, wt, qkv, att, att2, tqkv, A, smask, LS,
    ag_s, ag_r, fw_s, fw_r, rs_s, rs_r, z_s, z_r, a_s, a_r, zw_s, zw_r, wg_s, wg_r, wf_s, wf_r,
    at_s, at_r, so_s, so_r, l_s, l_r, ld_sem, own_sem, wm_sem, put_sem, mixb,
):
    V, L, D = lat.shape
    nch = n_space // 2
    span = n_space * L
    NR = len(ROUNDS)
    NU = UNITS
    Lu, Lh, Dh = L // NU, L // 2, D // 2
    sp = lax.axis_index("space")
    fr = lax.axis_index("frame")
    core = sp % 2
    chip = sp // 2
    cx, cy = chip % nx, chip // nx
    FR = wto_hbm.shape[0]
    U = FR // n_space
    sc, tc = wq.shape[2], wt.shape[2]
    sib = {"space": chip * 2 + (1 - core)}

    def chip_at(i, j):
        return ((cy + ny - j) % ny) * nx + (cx + nx - i) % nx

    def chip_to(i, j):
        return ((cy + j) % ny) * nx + (cx + i) % nx

    def at(i, j):
        return j * nx + i - 1

    def drain(ref, sem):
        pltpu.make_async_copy(ref, ref, sem).wait()

    def rcopy(src, dst, s, r, dev):
        return pltpu.make_async_remote_copy(
            src_ref=src, dst_ref=dst, send_sem=s, recv_sem=r, device_id=dev, device_id_type=MESH
        )

    def dev_to(i, j):
        return {"space": chip_to(i, j) * 2 + core}

    chunks = wt.shape[0] * (wt.shape[1] // FREQ)
    ncol = wmod_hbm.shape[1] // tc
    mod_rounds = (ncol + chunks - 1) // chunks
    per = wt.shape[1] // FREQ

    def wm(k):
        q = k % chunks
        return pltpu.make_async_copy(
            wmod_hbm.at[:, pl.ds(k * tc, tc)],
            wt.at[q // per, pl.ds((q % per) * FREQ, FREQ)],
            wm_sem.at[q // per],
        )

    ld_lat = pltpu.make_async_copy(lat_hbm, lat, ld_sem.at[0])
    ld_wq = pltpu.make_async_copy(wq_hbm, wq, ld_sem.at[1])
    ld_wso = pltpu.make_async_copy(wso_hbm, wso.at[0], ld_sem.at[2])
    ld_wt = pltpu.make_async_copy(wt_hbm, wt, ld_sem.at[3])
    ld_wto = pltpu.make_async_copy(
        wto_hbm, WO.at[pl.ds(pl.multiple_of(fr * FR, FR), FR)], ld_sem.at[4]
    )
    ld_tgt = pltpu.make_async_copy(tgt_hbm, tgt, ld_sem.at[5])

    bar = pltpu.get_barrier_semaphore()
    for o in range(1, n_space * n_frame):
        to = (fr * n_space + sp + o) % (n_space * n_frame)
        pl.semaphore_signal(
            bar, inc=1, device_id={"frame": to // n_space, "space": to % n_space}, device_id_type=MESH
        )

    half = FREQ // 2
    lane = lax.broadcasted_iota(jnp.int32, (8, half), 1).astype(F32)
    rows8 = lax.broadcasted_iota(jnp.int32, (8, half), 0)
    steps = jnp.zeros((8, half), F32)
    for v in range(V):
        steps = jnp.where(rows8 == v, ts_ref[v].astype(F32), steps)
    angles = steps * jnp.exp(-math.log(10000.0) * lane / half)
    embed = jnp.concatenate([jnp.cos(angles), jnp.sin(angles)], -1).astype(BF16)

    def mod_chunk(k):
        q = k % chunks
        w = wt[q // per, pl.ds((q % per) * FREQ, FREQ), :]
        sec, col = (k * tc) // D, (k * tc) % D
        MOD[sec, :, col : col + tc] = jnp.dot(embed, w, preferred_element_type=F32)

    def mod(v, i):
        return MOD[i, v : v + 1, :]

    def send2(blk, ss, rs, h, i, j):
        if h == 0:
            src = blk(chip, 0) if j == 0 else blk(chip_at(i, 0), 0)
            dev = dev_to(i, 0) if j == 0 else dev_to(0, j)
        else:
            src = blk(chip, 1) if i == 0 else blk(chip_at(0, j), 1)
            dev = dev_to(0, j) if i == 0 else dev_to(i, 0)
        return rcopy(src, src, ss, rs, dev)

    def recv2(blk, ss, rs, h, i, j):
        slot = blk(chip_at(i, j), h)
        return rcopy(slot, slot, ss, rs, sib)

    OFFS = [(i, j) for j in range(ny) for i in range(nx)]
    FIRST = [(0, i, 0) for i in range(1, nx)] + [(1, 0, j) for j in range(1, ny)]

    def relays_of(h, i, j):
        if h == 0:
            return [(0, i, jj) for jj in range(1, ny)]
        return [(1, ii, j) for ii in range(1, nx)]

    SECOND = [(0, 0, j) for j in range(1, ny)] + [(1, i, 0) for i in range(1, nx)]
    OWN_SENDS = FIRST + SECOND
    THIRD = [(h, i, j) for h in range(2) for j in range(1, ny) for i in range(1, nx)]
    ALL = [(h, i, j) for h in range(2) for (i, j) in OFFS if (i, j) != (0, 0)]

    def tok(v):
        return lambda c, h: G.at[v, c, core, pl.ds(h * Lh, Lh)]

    def ag(v, h, i, j):
        return send2(tok(v), ag_s.at[v], ag_r.at[v, h, at(i, j)], h, i, j)

    def ag_in(v, h, i, j):
        return recv2(tok(v), ag_s.at[v], ag_r.at[v, h, at(i, j)], h, i, j)

    def fw(v, h, i, j):
        slot = G.at[v, chip_at(i, j), core, pl.ds(h * Lh, Lh)]
        return rcopy(slot, slot, fw_s.at[v], fw_r.at[v, min(j, 1)], sib)

    def unit(f, s, h):
        row = pl.multiple_of(f * FR + s * U, U)
        return WO.at[pl.ds(row, U), pl.ds(h * (D // 2), D // 2)]

    def wrow(o):
        return lambda c, h: unit((fr + o) % n_frame, c * 2 + core, h)

    def wg(o, h, i, j):
        return send2(wrow(o), wg_s.at[0], wg_r.at[o - 1, h, at(i, j)], h, i, j)

    def wg_in(o, h, i, j):
        return recv2(wrow(o), wg_s.at[0], wg_r.at[o - 1, h, at(i, j)], h, i, j)

    def wf(o, h, i, j):
        slot = unit((fr + o) % n_frame, chip_at(i, j) * 2 + core, h)
        return rcopy(slot, slot, wf_s.at[0], wf_r.at[0], sib)

    def piece(r):
        a, n = ROUNDS[r]
        return pl.ds(a * L // 16, n * L // 16)

    def side(h):
        return pl.ds(h * Dh, Dh)

    def rs(v, r, h, i, j, first):
        src = G.at[v, chip_to(i, j), core, piece(r), side(h)]
        if h == 0:
            dev = dev_to(i, 0) if first else dev_to(0, j)
        else:
            dev = dev_to(0, j) if first else dev_to(i, 0)
        return rcopy(
            src, R.at[v, h, at(i, j), piece(r)], rs_s.at[v], rs_r.at[v, r, h, at(i, j)], dev
        )

    def rs_first(h):
        if h == 0:
            far = [(i, j) for i in range(1, nx) for j in range(1, ny)]
            near = [(i, 0) for i in range(1, nx)]
        else:
            far = [(i, j) for j in range(1, ny) for i in range(1, nx)]
            near = [(0, j) for j in range(1, ny)]
        return far, near

    def hblk(v, r, f):
        return H.at[v, f, piece(r)]

    def zsend(v, r, d, s):
        f = fr - s if d == 0 else fr + s
        to = fr + 1 if d == 0 else fr - 1
        blk = hblk(v, r, f)
        return rcopy(blk, blk, z_s.at[v, r, d, s], z_r.at[v, r, d, s], {"frame": to})

    def zin(v, r, d, s):
        f = fr - s if d == 0 else fr + s
        blk = hblk(v, r, f)
        return rcopy(blk, blk, z_s.at[v, r, d, s - 1], z_r.at[v, r, d, s - 1], sib)

    def wunit(f):
        return WO.at[pl.ds(pl.multiple_of(f * FR + sp * U, U), U)]

    def zwsend(d, s):
        f = fr - s if d == 0 else fr + s
        to = fr + 1 if d == 0 else fr - 1
        src = wto_hbm.at[pl.ds(pl.multiple_of(sp * U, U), U)] if s == 0 else wunit(f)
        return rcopy(src, wunit(f), zw_s.at[d, s], zw_r.at[d, s], {"frame": to})

    def zwin(d, s):
        f = fr - s if d == 0 else fr + s
        return rcopy(wunit(f), wunit(f), zw_s.at[d, s - 1], zw_r.at[d, s - 1], sib)

    def has(d, s):
        return fr >= s if d == 0 else fr + s < n_frame

    def sends(d, s):
        if d == 0:
            return (fr >= s) & (fr + 1 < n_frame)
        return (fr + s < n_frame) & (fr >= 1)

    def line_step(send, arrive, s):
        for d in range(2):
            if s > 0:
                pl.when(has(d, s))(lambda d=d: arrive(d, s).wait_recv())
            if s < n_frame - 1:
                pl.when(sends(d, s))(lambda d=d: send(d, s).start())

    def line_end(send):
        for s in range(n_frame - 1):
            for d in range(2):
                pl.when(sends(d, s))(lambda d=d, s=s: send(d, s).wait_send())

    def zstep(v, r, s):
        line_step(functools.partial(zsend, v, r), functools.partial(zin, v, r), s)

    def zwstep(s):
        line_step(zwsend, zwin, s)

    def ax(v, u, o):
        cols = pl.ds(pl.multiple_of(fr * tc, tc), tc)
        dst = (fr + o) % n_frame
        rows = pl.ds(u * Lu, Lu)
        return rcopy(
            A.at[v, dst, rows], C.at[v, rows, cols], a_s.at[0], a_r.at[0], {"frame": dst}
        )

    def attx(v):
        return rcopy(att.at[v, :, 1 - core], att2.at[v], at_s.at[v], at_r.at[v], sib)

    wso_x = rcopy(wso_hbm, wso.at[1], so_s.at[0], so_r.at[0], sib)

    ND = n_space * n_frame
    me = fr * n_space + sp

    def ls(o):
        to = (me + o) % ND
        return rcopy(
            LS.at[me], LS.at[me], l_s.at[0], l_r.at[0],
            {"frame": to // n_space, "space": to % n_space},
        )

    def norm_chip(v, c, slot):
        for e in range(2):
            x = norm_mod(G[v, c, e].astype(F32), mod(v, 0), mod(v, 1))
            X[pl.ds(slot * 2 * L + e * L, L)] = x

    def masks():
        nt = tiles_ref.shape[1]
        qt = lax.broadcasted_iota(jnp.int32, (nt, nt), 0)
        kt = lax.broadcasted_iota(jnp.int32, (nt, nt), 1)
        ids = (
            lax.broadcasted_iota(jnp.int32, (span, nt), 0) // TILE
            == lax.broadcasted_iota(jnp.int32, (span, nt), 1)
        ).astype(BF16)
        for v in range(V):
            ok = ((tiles_ref[v] == 1) & (kt < valid_ref[v, 1])) | (qt == kt)
            rows = jnp.dot(ids, ok.astype(BF16), preferred_element_type=F32).astype(BF16)
            full = lax.dot_general(rows, ids, (((1,), (1,)), ((), ())), preferred_element_type=F32)
            smask[v] = jnp.where(full > 0.5, 0.0, -1e30).astype(BF16)

    QB = 256
    XB = X.shape[0]
    pc = XB // (2 * L)

    def spatial_qkv(m):
        def step(j, _):
            qkv[j, pl.ds(pl.multiple_of(m * XB, XB), XB), :] = jnp.dot(
                X[...], wq[j], preferred_element_type=F32
            ).astype(BF16)
            return 0

        lax.fori_loop(0, 3, step, 0)

    def spatial_att(v):
        mt = QB // (2 * L)

        def step(i, _):
            rows = pl.ds(pl.multiple_of(i * QB, QB), QB)
            bias = smask[v, rows, :].astype(F32)
            for h in range(sc // HEAD_DIM):
                hs = slice(h * HEAD_DIM, (h + 1) * HEAD_DIM)
                out = attend(qkv[0, rows, hs], qkv[1, :, hs], qkv[2, :, hs], bias)
                att[v, pl.ds(i * mt, mt), :, :, hs] = out.reshape(mt, 2, L, HEAD_DIM)
            return 0

        lax.fori_loop(0, span // QB, step, 0)

    CB = 512

    def spatial_out(v):
        def step(i, _):
            cols = pl.ds(pl.multiple_of(i * CB, CB), CB)
            mine = att[v, :, core].reshape(nch * L, sc)
            other = att2[v].reshape(nch * L, sc)
            t = jnp.dot(mine, wso[0, :, cols], preferred_element_type=F32)
            t = t + jnp.dot(other, wso[1, :, cols], preferred_element_type=F32)
            G[v, :, core, :, cols] = t.astype(BF16).reshape(nch, L, CB)
            return 0

        lax.fori_loop(0, D // CB, step, 0)

    def rs_start(v, r):
        for k in range(2):
            for h in range(2):
                for i, j in rs_first(h)[k]:
                    rs(v, r, h, i, j, True).start()

    def rs_relay(v, r):
        for h in range(2):
            for b in range(1, ny if h == 0 else nx):
                if h == 0:
                    srcs, i, j = [(i, b) for i in range(1, nx)], 0, b
                else:
                    srcs, i, j = [(b, j) for j in range(1, ny)], b, 0
                c = chip_to(i, j)
                total = G[v, c, core, piece(r), side(h)].astype(F32)
                for a in srcs:
                    rs(v, r, h, a[0], a[1], True).wait_recv()
                    total = total + R[v, h, at(a[0], a[1]), piece(r)].astype(F32)
                G[v, c, core, piece(r), side(h)] = total.astype(BF16)
                rs(v, r, h, i, j, False).start()

    def finish(v, r):
        rows = piece(r)
        parts = []
        for h in range(2):
            so = G[v, chip, core, rows, side(h)].astype(F32)
            if h == 0:
                order = [(i, 0) for i in range(1, nx)] + [(0, j) for j in range(1, ny)]
            else:
                order = [(0, j) for j in range(1, ny)] + [(i, 0) for i in range(1, nx)]
            for i, j in order:
                rs(v, r, h, i, j, True).wait_recv()
                so = so + R[v, h, at(i, j), rows].astype(F32)
            parts.append(so)
        so = jnp.concatenate(parts, -1)
        x1 = (lat[v, rows].astype(F32) + mod(v, 2) * so).astype(BF16)
        x1_ref[v, rows] = x1
        H[v, fr, rows] = norm_mod(x1.astype(F32), mod(v, 3), mod(v, 4))
        zstep(v, r, 0)

    def temporal(v, u):
        NB = 256
        nn = tc // NB
        tl = n_frame * Lu
        rows = slice(u * Lu, (u + 1) * Lu)

        def step(i, _):
            j, n = i // nn, i % nn
            cols = pl.ds(pl.multiple_of(n * NB, NB), NB)
            x = H[v, :, rows, :].reshape(tl, D)
            tqkv[j, :, cols] = jnp.dot(x, wt[j, :, cols], preferred_element_type=F32).astype(BF16)
            return 0

        lax.fori_loop(0, 3 * nn, step, 0)
        q = lax.broadcasted_iota(jnp.int32, (tl, tl), 0)
        k = lax.broadcasted_iota(jnp.int32, (tl, tl), 1)
        ok = (q % Lu == k % Lu) & ((k // Lu < valid_ref[v, 0]) | (q // Lu == k // Lu))
        bias = jnp.where(ok, 0.0, -1e30)
        for h in range(tc // HEAD_DIM):
            hs = slice(h * HEAD_DIM, (h + 1) * HEAD_DIM)
            out = attend(tqkv[0, :, hs], tqkv[1, :, hs], tqkv[2, :, hs], bias)
            A[v, :, rows, hs] = out.reshape(n_frame, Lu, HEAD_DIM)
        for o in range(1, n_frame):
            ax(v, u, o).start()
        C[v, rows, pl.ds(pl.multiple_of(fr * tc, tc), tc)] = A[v, fr, rows]

    def load_mod(ks):
        for k in ks:
            wm(k).start()

    def take_mod(ks):
        for q in sorted({k % chunks // per for k in ks}):
            n = sum(1 for k in ks if k % chunks // per == q)
            drain(wt.at[q, pl.ds(0, n * FREQ)], wm_sem.at[q])
        for k in ks:
            mod_chunk(k)

    def gather_first(v):
        for h, i, j in FIRST:
            ag_in(v, h, i, j).wait_recv()
            for t in relays_of(h, i, j):
                ag(v, *t).start()
            fw(v, h, i, j).start()

    def gather_second(v):
        for h, i, j in SECOND:
            ag_in(v, h, i, j).wait_recv()
            fw(v, h, i, j).start()

    def gather_third(v):
        for h, i, j in THIRD:
            ag_in(v, h, i, j).wait_recv()
            fw(v, h, i, j).start()

    def own_load(v):
        return pltpu.make_async_copy(lat_hbm.at[v], G.at[v, chip, core], own_sem.at[v])

    def gather_own(v):
        for t in OWN_SENDS:
            ag(v, *t).start()
        for h in range(2):
            fw(v, h, 0, 0).start()

    def gather_end(v):
        n = len(ALL) // 2
        drain(G.at[v, pl.ds(0, n), core], ag_s.at[v])
        drain(G.at[v, :, core], fw_s.at[v])

    def near_qkv(v):
        drain(G.at[v, pl.ds(0, nx), 1 - core], fw_r.at[v, 0])
        for b in range(nx // pc):
            for i in range(pc):
                norm_chip(v, cy * nx + b * pc + i, i)
            if v == 0 and b == 0:
                ld_wq.wait()
            spatial_qkv(cy * (nx // pc) + b)

    def far_qkv(v):
        drain(G.at[v, pl.ds(0, nx * (ny - 1)), 1 - core], fw_r.at[v, 1])
        for j in range(1, ny):
            row = (cy + j) % ny
            for b in range(nx // pc):
                for i in range(pc):
                    norm_chip(v, row * nx + b * pc + i, i)
                spatial_qkv(row * (nx // pc) + b)

    def attention(v):
        spatial_att(v)
        attx(v).start()

    def project(v):
        gather_end(v)
        if v == 0:
            ld_wso.wait()
            wso_x.wait_recv()
        attx(v).wait_recv()
        spatial_out(v)

    def weights_own(o, part):
        for t in FIRST if part == 0 else SECOND:
            wg(o, *t).start()
        if part == 0:
            for h in range(2):
                wf(o, h, 0, 0).start()

    def weights_first(o):
        for h, i, j in FIRST:
            wg_in(o, h, i, j).wait_recv()
            for t in relays_of(h, i, j):
                wg(o, *t).start()
            wf(o, h, i, j).start()

    def weights_rest(o):
        for h, i, j in SECOND + THIRD:
            wg_in(o, h, i, j).wait_recv()
            wf(o, h, i, j).start()

    def late(v, r):
        for s in range(3, n_frame):
            zstep(v, r, s)

    ld_own = [own_load(v) for v in range(V)]
    ld_own[0].start()
    load_mod(range(min(chunks, ncol)))
    ld_own[1].start()
    ld_wq.start()
    ld_own[0].wait()
    pl.semaphore_wait(bar, n_space * n_frame - 1)
    gather_own(0)
    zwstep(0)
    wso_x.start()
    masks()
    gather_first(0)
    ld_own[1].wait()
    gather_own(1)
    ld_wso.start()
    ld_lat.start()
    take_mod(range(min(chunks, ncol)))
    for m in range(1, mod_rounds):
        ks = range(m * chunks, min((m + 1) * chunks, ncol))
        load_mod(ks)
        take_mod(ks)
    ld_wt.start()
    ld_wto.start()
    ld_tgt.start()
    zwstep(1)
    gather_second(0)
    near_qkv(0)
    gather_third(0)
    far_qkv(0)
    gather_first(1)
    attention(0)
    zwstep(2)
    project(0)
    rs_start(0, 0)
    rs_start(0, 1)
    ld_lat.wait()
    gather_second(1)
    near_qkv(1)
    rs_relay(0, 0)
    rs_relay(0, 1)
    rs_start(0, 2)
    gather_third(1)
    far_qkv(1)
    finish(0, 0)
    finish(0, 1)
    rs_relay(0, 2)
    zstep(0, 0, 1)
    attention(1)
    zstep(0, 1, 1)
    project(1)
    rs_start(1, 0)
    rs_start(1, 1)
    zstep(0, 0, 2)
    finish(0, 2)
    zstep(0, 1, 2)
    rs_relay(1, 0)
    rs_relay(1, 1)
    rs_start(1, 2)
    for s in range(3, n_frame):
        zwstep(s)
    finish(1, 0)
    zstep(0, 2, 1)
    finish(1, 1)
    rs_relay(1, 2)
    for o in (1, 2):
        weights_own(o, 0)
        weights_own(o, 1)
    zstep(0, 2, 2)
    finish(1, 2)
    zstep(1, 0, 1)
    zstep(1, 1, 1)
    zstep(1, 2, 1)
    weights_first(1)
    for o in range(3, n_frame):
        weights_own(o, 0)
        weights_own(o, 1)
    late(0, 0)
    late(0, 1)
    ld_wt.wait()
    temporal(0, 0)
    zstep(1, 0, 2)
    zstep(1, 1, 2)
    zstep(1, 2, 2)
    late(0, 2)
    temporal(0, 1)
    weights_rest(1)
    weights_first(2)
    late(1, 0)
    late(1, 1)
    temporal(1, 0)
    for o in range(3, n_frame):
        weights_first(o)
    late(1, 2)
    temporal(1, 1)
    for o in range(2, n_frame):
        weights_rest(o)

    wrows = (n_frame - 1) * 2 * U
    drain(WO.at[pl.ds(0, wrows * nch), pl.ds(0, Dh)], wf_r.at[0])
    drain(C.at[:, :, pl.ds(0, (n_frame - 1) * tc)], a_r.at[0])
    ld_tgt.wait()
    ld_wto.wait()

    def out_step(i, total):
        cols = pl.ds(pl.multiple_of(i * CB, CB), CB)
        a = C[...].reshape(V * L, n_frame * tc)
        acc = jnp.dot(a, WO[:, cols], preferred_element_type=F32)
        part = []
        for v in range(V):
            gate = MOD[5, v : v + 1, cols]
            m = x1_ref[v, :, cols].astype(F32) + gate * acc[v * L : (v + 1) * L]
            m = m.astype(BF16)
            mixb[v, :, cols] = m
            diff = m.astype(F32) - tgt[v, :, cols].astype(F32)
            part.append(jnp.sum(diff * diff, -1, keepdims=True))
        return total + jnp.concatenate(part, 0)

    squares = lax.fori_loop(0, D // CB, out_step, jnp.zeros((V * L, 1), F32)) * (1.0 / D)
    place = sp * L + lax.broadcasted_iota(jnp.int32, (L, 1), 0)
    here = jnp.zeros((1, 1), F32)
    count = jnp.int32(0)
    for v in range(V):
        keep = (place // TILE < valid_ref[v, 1]) & (fr < valid_ref[v, 0])
        here = here + jnp.sum(
            jnp.where(keep, squares[v * L : (v + 1) * L], 0.0), 0, keepdims=True
        )
        count = count + valid_ref[v, 0] * valid_ref[v, 1]
    put = pltpu.make_async_copy(mixb, mixed_ref, put_sem.at[0])
    put.start()
    LS[me] = jnp.broadcast_to(here, (8, 128))
    for o in range(1, ND):
        ls(o).start()
    drain(LS.at[pl.ds(0, ND - 1)], l_r.at[0])
    loss_ref[0, 0] = jnp.sum(jnp.sum(LS[...], 0)[0:1, 0:1]) / (count.astype(F32) * TILE)

    put.wait()
    wso_x.wait_send()
    for v in range(V):
        attx(v).wait_send()
        drain(G.at[v, pl.ds(0, nch - 1), core], rs_s.at[v])
        for r in range(NR):
            line_end(functools.partial(zsend, v, r))
    line_end(zwsend)
    drain(C.at[:, :, pl.ds(0, (n_frame - 1) * tc)], a_s.at[0])
    drain(WO.at[pl.ds(0, wrows * (nch - 1)), pl.ds(0, Dh)], wg_s.at[0])
    drain(WO.at[pl.ds(0, wrows * nch), pl.ds(0, Dh)], wf_s.at[0])
    drain(LS.at[pl.ds(0, ND - 1)], l_s.at[0])


def run_kernel(timesteps, valid, tile_mask, latents, w_mod, w_sqkv, w_sout, w_tqkv, w_tout, target):
    V, L, D = latents.shape
    n_space = lax.axis_size("space")
    n_frame = lax.axis_size("frame")
    nch = n_space // 2
    ny = 2 if nch % 2 == 0 else 1
    nx = nch // ny
    NR = len(ROUNDS)
    sc, tc = w_sqkv.shape[2], w_tqkv.shape[2]
    span = n_space * L
    tl = n_frame * L // UNITS
    far = nx * ny - 1
    n1 = n_frame - 1
    dma = pltpu.SemaphoreType.DMA
    vm = pl.BlockSpec(memory_space=pltpu.VMEM)
    sm = pl.BlockSpec(memory_space=pltpu.SMEM)
    hbm = pl.BlockSpec(memory_space=pl.ANY)
    return pl.pallas_call(
        functools.partial(kernel, n_space, n_frame, nx, ny),
        out_shape=(
            jax.ShapeDtypeStruct((V, L, D), BF16),
            jax.ShapeDtypeStruct((1, 1), F32),
        ),
        in_specs=[sm, sm, vm] + [hbm] * 7,
        out_specs=(hbm, sm),
        scratch_shapes=[
            pltpu.VMEM((V, L, D), BF16),
            pltpu.VMEM((V, L, D), BF16),
            pltpu.VMEM((6, 8, D), F32),
            pltpu.VMEM((V, nch, 2, L, D), BF16),
            pltpu.VMEM((256, D), BF16),
            pltpu.VMEM((V, 2, far, L, D // 2), BF16),
            pltpu.VMEM((V, n_frame, L, D), BF16),
            pltpu.VMEM((V, L, n_frame * tc), BF16),
            pltpu.VMEM((V, L, D), BF16),
            pltpu.VMEM((n_frame * w_tout.shape[0], D), BF16),
            pltpu.VMEM(w_sqkv.shape, BF16),
            pltpu.VMEM((2,) + w_sout.shape, BF16),
            pltpu.VMEM(w_tqkv.shape, BF16),
            pltpu.VMEM((3, span, sc), BF16),
            pltpu.VMEM((V, nch, 2, L, sc), BF16),
            pltpu.VMEM((V, nch, L, sc), BF16),
            pltpu.VMEM((3, tl, tc), BF16),
            pltpu.VMEM((V, n_frame, L, tc), BF16),
            pltpu.VMEM((V, span, span), BF16),
            pltpu.VMEM((n_space * n_frame, 8, 128), F32),
            dma((V,)), dma((V, 2, far)), dma((V,)), dma((V, 2)),
            dma((V,)), dma((V, NR, 2, far)),
            dma((V, NR, 2, n1)), dma((V, NR, 2, n1)),
            dma((1,)), dma((1,)),
            dma((2, n1)), dma((2, n1)),
            dma((1,)), dma((n1, 2, far)), dma((1,)), dma((1,)),
            dma((V,)), dma((V,)), dma((1,)), dma((1,)),
            dma((1,)), dma((1,)),
            dma((6,)), dma((V,)), dma((3,)), dma((1,)),
            pltpu.VMEM((V, L, D), BF16),
        ],
        compiler_params=pltpu.CompilerParams(
            collective_id=0, has_side_effects=True, vmem_limit_bytes=61 * 1024 * 1024
        ),
        cost_estimate=pl.CostEstimate(
            flops=14_000_000_000, bytes_accessed=35_000_000, transcendentals=3_000_000
        ),
        name="block",
    )(timesteps, valid, tile_mask, latents, w_mod, w_sqkv, w_sout, w_tqkv, w_tout, target)


def shards(latents, target, timesteps, valid, tile_mask, w_mod, w_sqkv, w_sout, w_tqkv, w_tout):
    videos, frames_dev, span_dev, width = latents.shape
    shape = (videos, span_dev, width)
    mixed, loss = run_kernel(
        timesteps, valid, tile_mask, latents.reshape(shape), w_mod,
        w_sqkv, w_sout, w_tqkv, w_tout, target.reshape(shape),
    )
    return (mixed.reshape(latents.shape), loss.reshape(()))


def solution(mesh):
    return jax.shard_map(
        shards,
        mesh=mesh,
        in_specs=(
            P(None, "frame", "space", None),
            P(None, "frame", "space", None),
            P(),
            P(),
            P(),
            P(),
            P(None, None, "space"),
            P("space", None),
            P(None, None, "frame"),
            P("frame", None),
        ),
        out_specs=(P(None, "frame", "space", None), P()),
        check_vma=False,
    )
```

```python
import functools
import math

import jax
import jax.numpy as jnp
from jax import lax
from jax.experimental import pallas as pl
from jax.experimental.pallas import tpu as pltpu
from jax.sharding import PartitionSpec as P

HEAD_DIM = 128
FREQ = 256
TILE = 32
ROUNDS = ((0, 4), (4, 4), (8, 8))
UNITS = 2
MESH = pl.DeviceIdType.MESH
F32 = jnp.float32
BF16 = jnp.bfloat16


def norm_mod(values, shift, scale):
    mean = jnp.mean(values, -1, keepdims=True)
    centred = values - mean
    var = jnp.mean(centred * centred, -1, keepdims=True)
    return (centred * lax.rsqrt(var + 1e-06) * (1.0 + scale) + shift).astype(BF16)


def attend(query, keys, values, bias):
    scores = lax.dot_general(query, keys, (((1,), (1,)), ((), ())), preferred_element_type=F32)
    scores = scores * (math.log2(math.e) / math.sqrt(HEAD_DIM)) + bias
    top = jnp.max(scores, -1, keepdims=True)
    weights = jnp.exp2(scores - top)
    total = jnp.sum(weights, -1, keepdims=True)
    out = jnp.dot(weights.astype(BF16), values, preferred_element_type=F32)
    return (out * (1.0 / total)).astype(BF16)


def kernel(
    n_space, n_frame, nx, ny,
    ts_ref, valid_ref, tiles_ref, lat_hbm, wmod_hbm, wq_hbm, wso_hbm, wt_hbm, wto_hbm, tgt_hbm,
    mixed_ref, loss_ref,
    lat, tgt, MOD, G, X, R, H, C, x1_ref, WO, wq, wso, wt, qkv, att, att2, tqkv, A, smask, LS,
    ag_s, ag_r, fw_s, fw_r, rs_s, rs_r, z_s, z_r, a_s, a_r, zw_s, zw_r, wg_s, wg_r, wf_s, wf_r,
    at_s, at_r, so_s, so_r, l_s, l_r, ld_sem, own_sem, wm_sem, put_sem, mixb,
):
    V, L, D = lat.shape
    nch = n_space // 2
    span = n_space * L
    NR = len(ROUNDS)
    NU = UNITS
    Lu, Lh, Dh = L // NU, L // 2, D // 2
    sp = lax.axis_index("space")
    fr = lax.axis_index("frame")
    core = sp % 2
    chip = sp // 2
    cx, cy = chip % nx, chip // nx
    FR = wto_hbm.shape[0]
    U = FR // n_space
    sc, tc = wq.shape[2], wt.shape[2]
    sib = {"space": chip * 2 + (1 - core)}

    def chip_at(i, j):
        return ((cy + ny - j) % ny) * nx + (cx + nx - i) % nx

    def chip_to(i, j):
        return ((cy + j) % ny) * nx + (cx + i) % nx

    def at(i, j):
        return j * nx + i - 1

    def drain(ref, sem):
        pltpu.make_async_copy(ref, ref, sem).wait()

    def rcopy(src, dst, s, r, dev):
        return pltpu.make_async_remote_copy(
            src_ref=src, dst_ref=dst, send_sem=s, recv_sem=r, device_id=dev, device_id_type=MESH
        )

    def dev_to(i, j):
        return {"space": chip_to(i, j) * 2 + core}

    chunks = wt.shape[0] * (wt.shape[1] // FREQ)
    ncol = wmod_hbm.shape[1] // tc
    mod_rounds = (ncol + chunks - 1) // chunks
    per = wt.shape[1] // FREQ

    def wm(k):
        q = k % chunks
        return pltpu.make_async_copy(
            wmod_hbm.at[:, pl.ds(k * tc, tc)],
            wt.at[q // per, pl.ds((q % per) * FREQ, FREQ)],
            wm_sem.at[q // per],
        )

    ld_lat = pltpu.make_async_copy(lat_hbm, lat, ld_sem.at[0])
    ld_wq = pltpu.make_async_copy(wq_hbm, wq, ld_sem.at[1])
    ld_wso = pltpu.make_async_copy(wso_hbm, wso.at[0], ld_sem.at[2])
    ld_wt = pltpu.make_async_copy(wt_hbm, wt, ld_sem.at[3])
    ld_wto = pltpu.make_async_copy(
        wto_hbm, WO.at[pl.ds(pl.multiple_of(fr * FR, FR), FR)], ld_sem.at[4]
    )
    ld_tgt = pltpu.make_async_copy(tgt_hbm, tgt, ld_sem.at[5])

    bar = pltpu.get_barrier_semaphore()
    for o in range(1, n_space * n_frame):
        to = (fr * n_space + sp + o) % (n_space * n_frame)
        pl.semaphore_signal(
            bar, inc=1, device_id={"frame": to // n_space, "space": to % n_space}, device_id_type=MESH
        )

    half = FREQ // 2
    lane = lax.broadcasted_iota(jnp.int32, (8, half), 1).astype(F32)
    rows8 = lax.broadcasted_iota(jnp.int32, (8, half), 0)
    steps = jnp.zeros((8, half), F32)
    for v in range(V):
        steps = jnp.where(rows8 == v, ts_ref[v].astype(F32), steps)
    angles = steps * jnp.exp(-math.log(10000.0) * lane / half)
    embed = jnp.concatenate([jnp.cos(angles), jnp.sin(angles)], -1).astype(BF16)

    def mod_chunk(k):
        q = k % chunks
        w = wt[q // per, pl.ds((q % per) * FREQ, FREQ), :]
        sec, col = (k * tc) // D, (k * tc) % D
        MOD[sec, :, col : col + tc] = jnp.dot(embed, w, preferred_element_type=F32)

    def mod(v, i):
        return MOD[i, v : v + 1, :]

    def send2(blk, ss, rs, h, i, j):
        if h == 0:
            src = blk(chip, 0) if j == 0 else blk(chip_at(i, 0), 0)
            dev = dev_to(i, 0) if j == 0 else dev_to(0, j)
        else:
            src = blk(chip, 1) if i == 0 else blk(chip_at(0, j), 1)
            dev = dev_to(0, j) if i == 0 else dev_to(i, 0)
        return rcopy(src, src, ss, rs, dev)

    def recv2(blk, ss, rs, h, i, j):
        slot = blk(chip_at(i, j), h)
        return rcopy(slot, slot, ss, rs, sib)

    OFFS = [(i, j) for j in range(ny) for i in range(nx)]
    FIRST = [(0, i, 0) for i in range(1, nx)] + [(1, 0, j) for j in range(1, ny)]

    def relays_of(h, i, j):
        if h == 0:
            return [(0, i, jj) for jj in range(1, ny)]
        return [(1, ii, j) for ii in range(1, nx)]

    SECOND = [(0, 0, j) for j in range(1, ny)] + [(1, i, 0) for i in range(1, nx)]
    OWN_SENDS = FIRST + SECOND
    THIRD = [(h, i, j) for h in range(2) for j in range(1, ny) for i in range(1, nx)]
    ALL = [(h, i, j) for h in range(2) for (i, j) in OFFS if (i, j) != (0, 0)]

    def tok(v):
        return lambda c, h: G.at[v, c, core, pl.ds(h * Lh, Lh)]

    def ag(v, h, i, j):
        return send2(tok(v), ag_s.at[v], ag_r.at[v, h, at(i, j)], h, i, j)

    def ag_in(v, h, i, j):
        return recv2(tok(v), ag_s.at[v], ag_r.at[v, h, at(i, j)], h, i, j)

    def fw(v, h, i, j):
        slot = G.at[v, chip_at(i, j), core, pl.ds(h * Lh, Lh)]
        return rcopy(slot, slot, fw_s.at[v], fw_r.at[v, min(j, 1)], sib)

    def unit(f, s, h):
        row = pl.multiple_of(f * FR + s * U, U)
        return WO.at[pl.ds(row, U), pl.ds(h * (D // 2), D // 2)]

    def wrow(o):
        return lambda c, h: unit((fr + o) % n_frame, c * 2 + core, h)

    def wg(o, h, i, j):
        return send2(wrow(o), wg_s.at[0], wg_r.at[o - 1, h, at(i, j)], h, i, j)

    def wg_in(o, h, i, j):
        return recv2(wrow(o), wg_s.at[0], wg_r.at[o - 1, h, at(i, j)], h, i, j)

    def wf(o, h, i, j):
        slot = unit((fr + o) % n_frame, chip_at(i, j) * 2 + core, h)
        return rcopy(slot, slot, wf_s.at[0], wf_r.at[0], sib)

    def piece(r):
        a, n = ROUNDS[r]
        return pl.ds(a * L // 16, n * L // 16)

    def side(h):
        return pl.ds(h * Dh, Dh)

    def rs(v, r, h, i, j, first):
        src = G.at[v, chip_to(i, j), core, piece(r), side(h)]
        if h == 0:
            dev = dev_to(i, 0) if first else dev_to(0, j)
        else:
            dev = dev_to(0, j) if first else dev_to(i, 0)
        return rcopy(
            src, R.at[v, h, at(i, j), piece(r)], rs_s.at[v], rs_r.at[v, r, h, at(i, j)], dev
        )

    def rs_first(h):
        if h == 0:
            far = [(i, j) for i in range(1, nx) for j in range(1, ny)]
            near = [(i, 0) for i in range(1, nx)]
        else:
            far = [(i, j) for j in range(1, ny) for i in range(1, nx)]
            near = [(0, j) for j in range(1, ny)]
        return far, near

    def hblk(v, r, f):
        return H.at[v, f, piece(r)]

    def zsend(v, r, d, s):
        f = fr - s if d == 0 else fr + s
        to = fr + 1 if d == 0 else fr - 1
        blk = hblk(v, r, f)
        return rcopy(blk, blk, z_s.at[v, r, d, s], z_r.at[v, r, d, s], {"frame": to})

    def zin(v, r, d, s):
        f = fr - s if d == 0 else fr + s
        blk = hblk(v, r, f)
        return rcopy(blk, blk, z_s.at[v, r, d, s - 1], z_r.at[v, r, d, s - 1], sib)

    def wunit(f):
        return WO.at[pl.ds(pl.multiple_of(f * FR + sp * U, U), U)]

    def zwsend(d, s):
        f = fr - s if d == 0 else fr + s
        to = fr + 1 if d == 0 else fr - 1
        src = wto_hbm.at[pl.ds(pl.multiple_of(sp * U, U), U)] if s == 0 else wunit(f)
        return rcopy(src, wunit(f), zw_s.at[d, s], zw_r.at[d, s], {"frame": to})

    def zwin(d, s):
        f = fr - s if d == 0 else fr + s
        return rcopy(wunit(f), wunit(f), zw_s.at[d, s - 1], zw_r.at[d, s - 1], sib)

    def has(d, s):
        return fr >= s if d == 0 else fr + s < n_frame

    def sends(d, s):
        if d == 0:
            return (fr >= s) & (fr + 1 < n_frame)
        return (fr + s < n_frame) & (fr >= 1)

    def line_step(send, arrive, s):
        for d in range(2):
            if s > 0:
                pl.when(has(d, s))(lambda d=d: arrive(d, s).wait_recv())
            if s < n_frame - 1:
                pl.when(sends(d, s))(lambda d=d: send(d, s).start())

    def line_end(send):
        for s in range(n_frame - 1):
            for d in range(2):
                pl.when(sends(d, s))(lambda d=d, s=s: send(d, s).wait_send())

    def zstep(v, r, s):
        line_step(functools.partial(zsend, v, r), functools.partial(zin, v, r), s)

    def zwstep(s):
        line_step(zwsend, zwin, s)

    def ax(v, u, o):
        cols = pl.ds(pl.multiple_of(fr * tc, tc), tc)
        dst = (fr + o) % n_frame
        rows = pl.ds(u * Lu, Lu)
        return rcopy(
            A.at[v, dst, rows], C.at[v, rows, cols], a_s.at[0], a_r.at[0], {"frame": dst}
        )

    def attx(v):
        return rcopy(att.at[v, :, 1 - core], att2.at[v], at_s.at[v], at_r.at[v], sib)

    wso_x = rcopy(wso_hbm, wso.at[1], so_s.at[0], so_r.at[0], sib)

    ND = n_space * n_frame
    me = fr * n_space + sp

    def ls(o):
        to = (me + o) % ND
        return rcopy(
            LS.at[me], LS.at[me], l_s.at[0], l_r.at[0],
            {"frame": to // n_space, "space": to % n_space},
        )

    def norm_chip(v, c, slot):
        for e in range(2):
            x = norm_mod(G[v, c, e].astype(F32), mod(v, 0), mod(v, 1))
            X[pl.ds(slot * 2 * L + e * L, L)] = x

    def masks():
        nt = tiles_ref.shape[1]
        qt = lax.broadcasted_iota(jnp.int32, (nt, nt), 0)
        kt = lax.broadcasted_iota(jnp.int32, (nt, nt), 1)
        ids = (
            lax.broadcasted_iota(jnp.int32, (span, nt), 0) // TILE
            == lax.broadcasted_iota(jnp.int32, (span, nt), 1)
        ).astype(BF16)
        for v in range(V):
            ok = ((tiles_ref[v] == 1) & (kt < valid_ref[v, 1])) | (qt == kt)
            rows = jnp.dot(ids, ok.astype(BF16), preferred_element_type=F32).astype(BF16)
            full = lax.dot_general(rows, ids, (((1,), (1,)), ((), ())), preferred_element_type=F32)
            smask[v] = jnp.where(full > 0.5, 0.0, -1e30).astype(BF16)

    QB = 256
    XB = X.shape[0]
    pc = XB // (2 * L)

    def spatial_qkv(m):
        def step(j, _):
            qkv[j, pl.ds(pl.multiple_of(m * XB, XB), XB), :] = jnp.dot(
                X[...], wq[j], preferred_element_type=F32
            ).astype(BF16)
            return 0

        lax.fori_loop(0, 3, step, 0)

    def spatial_att(v):
        mt = QB // (2 * L)

        def step(i, _):
            rows = pl.ds(pl.multiple_of(i * QB, QB), QB)
            bias = smask[v, rows, :].astype(F32)
            for h in range(sc // HEAD_DIM):
                hs = slice(h * HEAD_DIM, (h + 1) * HEAD_DIM)
                out = attend(qkv[0, rows, hs], qkv[1, :, hs], qkv[2, :, hs], bias)
                att[v, pl.ds(i * mt, mt), :, :, hs] = out.reshape(mt, 2, L, HEAD_DIM)
            return 0

        lax.fori_loop(0, span // QB, step, 0)

    CB = 512

    def spatial_out(v):
        def step(i, _):
            cols = pl.ds(pl.multiple_of(i * CB, CB), CB)
            mine = att[v, :, core].reshape(nch * L, sc)
            other = att2[v].reshape(nch * L, sc)
            t = jnp.dot(mine, wso[0, :, cols], preferred_element_type=F32)
            t = t + jnp.dot(other, wso[1, :, cols], preferred_element_type=F32)
            G[v, :, core, :, cols] = t.astype(BF16).reshape(nch, L, CB)
            return 0

        lax.fori_loop(0, D // CB, step, 0)

    def rs_start(v, r):
        for k in range(2):
            for h in range(2):
                for i, j in rs_first(h)[k]:
                    rs(v, r, h, i, j, True).start()

    def rs_relay(v, r):
        for h in range(2):
            for b in range(1, ny if h == 0 else nx):
                if h == 0:
                    srcs, i, j = [(i, b) for i in range(1, nx)], 0, b
                else:
                    srcs, i, j = [(b, j) for j in range(1, ny)], b, 0
                c = chip_to(i, j)
                total = G[v, c, core, piece(r), side(h)].astype(F32)
                for a in srcs:
                    rs(v, r, h, a[0], a[1], True).wait_recv()
                    total = total + R[v, h, at(a[0], a[1]), piece(r)].astype(F32)
                G[v, c, core, piece(r), side(h)] = total.astype(BF16)
                rs(v, r, h, i, j, False).start()

    def finish(v, r):
        rows = piece(r)
        parts = []
        for h in range(2):
            so = G[v, chip, core, rows, side(h)].astype(F32)
            if h == 0:
                order = [(i, 0) for i in range(1, nx)] + [(0, j) for j in range(1, ny)]
            else:
                order = [(0, j) for j in range(1, ny)] + [(i, 0) for i in range(1, nx)]
            for i, j in order:
                rs(v, r, h, i, j, True).wait_recv()
                so = so + R[v, h, at(i, j), rows].astype(F32)
            parts.append(so)
        so = jnp.concatenate(parts, -1)
        x1 = (lat[v, rows].astype(F32) + mod(v, 2) * so).astype(BF16)
        x1_ref[v, rows] = x1
        H[v, fr, rows] = norm_mod(x1.astype(F32), mod(v, 3), mod(v, 4))
        zstep(v, r, 0)

    def temporal(v, u):
        NB = 256
        nn = tc // NB
        tl = n_frame * Lu
        rows = slice(u * Lu, (u + 1) * Lu)

        def step(i, _):
            j, n = i // nn, i % nn
            cols = pl.ds(pl.multiple_of(n * NB, NB), NB)
            x = H[v, :, rows, :].reshape(tl, D)
            tqkv[j, :, cols] = jnp.dot(x, wt[j, :, cols], preferred_element_type=F32).astype(BF16)
            return 0

        lax.fori_loop(0, 3 * nn, step, 0)
        q = lax.broadcasted_iota(jnp.int32, (tl, tl), 0)
        k = lax.broadcasted_iota(jnp.int32, (tl, tl), 1)
        ok = (q % Lu == k % Lu) & ((k // Lu < valid_ref[v, 0]) | (q // Lu == k // Lu))
        bias = jnp.where(ok, 0.0, -1e30)
        for h in range(tc // HEAD_DIM):
            hs = slice(h * HEAD_DIM, (h + 1) * HEAD_DIM)
            out = attend(tqkv[0, :, hs], tqkv[1, :, hs], tqkv[2, :, hs], bias)
            A[v, :, rows, hs] = out.reshape(n_frame, Lu, HEAD_DIM)
        for o in range(1, n_frame):
            ax(v, u, o).start()
        C[v, rows, pl.ds(pl.multiple_of(fr * tc, tc), tc)] = A[v, fr, rows]

    def load_mod(ks):
        for k in ks:
            wm(k).start()

    def take_mod(ks):
        for q in sorted({k % chunks // per for k in ks}):
            n = sum(1 for k in ks if k % chunks // per == q)
            drain(wt.at[q, pl.ds(0, n * FREQ)], wm_sem.at[q])
        for k in ks:
            mod_chunk(k)

    def gather_first(v):
        for h, i, j in FIRST:
            ag_in(v, h, i, j).wait_recv()
            for t in relays_of(h, i, j):
                ag(v, *t).start()
            fw(v, h, i, j).start()

    def gather_second(v):
        for h, i, j in SECOND:
            ag_in(v, h, i, j).wait_recv()
            fw(v, h, i, j).start()

    def gather_third(v):
        for h, i, j in THIRD:
            ag_in(v, h, i, j).wait_recv()
            fw(v, h, i, j).start()

    def own_load(v):
        return pltpu.make_async_copy(lat_hbm.at[v], G.at[v, chip, core], own_sem.at[v])

    def gather_own(v):
        for t in OWN_SENDS:
            ag(v, *t).start()
        for h in range(2):
            fw(v, h, 0, 0).start()

    def gather_end(v):
        n = len(ALL) // 2
        drain(G.at[v, pl.ds(0, n), core], ag_s.at[v])
        drain(G.at[v, :, core], fw_s.at[v])

    def near_qkv(v):
        drain(G.at[v, pl.ds(0, nx), 1 - core], fw_r.at[v, 0])
        for b in range(nx // pc):
            for i in range(pc):
                norm_chip(v, cy * nx + b * pc + i, i)
            if v == 0 and b == 0:
                ld_wq.wait()
            spatial_qkv(cy * (nx // pc) + b)

    def far_qkv(v):
        drain(G.at[v, pl.ds(0, nx * (ny - 1)), 1 - core], fw_r.at[v, 1])
        for j in range(1, ny):
            row = (cy + j) % ny
            for b in range(nx // pc):
                for i in range(pc):
                    norm_chip(v, row * nx + b * pc + i, i)
                spatial_qkv(row * (nx // pc) + b)

    def attention(v):
        spatial_att(v)
        attx(v).start()

    def project(v):
        gather_end(v)
        if v == 0:
            ld_wso.wait()
            wso_x.wait_recv()
        attx(v).wait_recv()
        spatial_out(v)

    def weights_own(o, part):
        for t in FIRST if part == 0 else SECOND:
            wg(o, *t).start()
        if part == 0:
            for h in range(2):
                wf(o, h, 0, 0).start()

    def weights_first(o):
        for h, i, j in FIRST:
            wg_in(o, h, i, j).wait_recv()
            for t in relays_of(h, i, j):
                wg(o, *t).start()
            wf(o, h, i, j).start()

    def weights_rest(o):
        for h, i, j in SECOND + THIRD:
            wg_in(o, h, i, j).wait_recv()
            wf(o, h, i, j).start()

    def late(v, r):
        for s in range(3, n_frame):
            zstep(v, r, s)

    ld_own = [own_load(v) for v in range(V)]
    ld_own[0].start()
    load_mod(range(min(chunks, ncol)))
    ld_own[1].start()
    ld_wq.start()
    ld_own[0].wait()
    pl.semaphore_wait(bar, n_space * n_frame - 1)
    gather_own(0)
    zwstep(0)
    wso_x.start()
    masks()
    gather_first(0)
    ld_own[1].wait()
    gather_own(1)
    ld_wso.start()
    ld_lat.start()
    take_mod(range(min(chunks, ncol)))
    for m in range(1, mod_rounds):
        ks = range(m * chunks, min((m + 1) * chunks, ncol))
        load_mod(ks)
        take_mod(ks)
    ld_wt.start()
    ld_wto.start()
    ld_tgt.start()
    zwstep(1)
    gather_second(0)
    near_qkv(0)
    gather_third(0)
    far_qkv(0)
    gather_first(1)
    attention(0)
    zwstep(2)
    project(0)
    rs_start(0, 0)
    rs_start(0, 1)
    ld_lat.wait()
    gather_second(1)
    near_qkv(1)
    rs_relay(0, 0)
    rs_relay(0, 1)
    rs_start(0, 2)
    gather_third(1)
    far_qkv(1)
    finish(0, 0)
    finish(0, 1)
    rs_relay(0, 2)
    zstep(0, 0, 1)
    attention(1)
    zstep(0, 1, 1)
    project(1)
    rs_start(1, 0)
    rs_start(1, 1)
    zstep(0, 0, 2)
    finish(0, 2)
    zstep(0, 1, 2)
    rs_relay(1, 0)
    rs_relay(1, 1)
    rs_start(1, 2)
    for s in range(3, n_frame):
        zwstep(s)
    finish(1, 0)
    zstep(0, 2, 1)
    finish(1, 1)
    rs_relay(1, 2)
    for o in (1, 2):
        weights_own(o, 0)
        weights_own(o, 1)
    zstep(0, 2, 2)
    finish(1, 2)
    zstep(1, 0, 1)
    zstep(1, 1, 1)
    zstep(1, 2, 1)
    weights_first(1)
    for o in range(3, n_frame):
        weights_own(o, 0)
        weights_own(o, 1)
    late(0, 0)
    late(0, 1)
    ld_wt.wait()
    temporal(0, 0)
    zstep(1, 0, 2)
    zstep(1, 1, 2)
    zstep(1, 2, 2)
    late(0, 2)
    temporal(0, 1)
    weights_rest(1)
    weights_first(2)
    late(1, 0)
    late(1, 1)
    temporal(1, 0)
    for o in range(3, n_frame):
        weights_first(o)
    for o in range(2, n_frame - 1):
        weights_rest(o)
    late(1, 2)
    temporal(1, 1)
    weights_rest(n_frame - 1)

    wrows = (n_frame - 1) * 2 * U
    drain(WO.at[pl.ds(0, wrows * nch), pl.ds(0, Dh)], wf_r.at[0])
    drain(C.at[:, :, pl.ds(0, (n_frame - 1) * tc)], a_r.at[0])
    ld_tgt.wait()
    ld_wto.wait()

    def out_step(i, total):
        cols = pl.ds(pl.multiple_of(i * CB, CB), CB)
        a = C[...].reshape(V * L, n_frame * tc)
        acc = jnp.dot(a, WO[:, cols], preferred_element_type=F32)
        part = []
        for v in range(V):
            gate = MOD[5, v : v + 1, cols]
            m = x1_ref[v, :, cols].astype(F32) + gate * acc[v * L : (v + 1) * L]
            m = m.astype(BF16)
            mixb[v, :, cols] = m
            diff = m.astype(F32) - tgt[v, :, cols].astype(F32)
            part.append(jnp.sum(diff * diff, -1, keepdims=True))
        return total + jnp.concatenate(part, 0)

    squares = lax.fori_loop(0, D // CB, out_step, jnp.zeros((V * L, 1), F32)) * (1.0 / D)
    place = sp * L + lax.broadcasted_iota(jnp.int32, (L, 1), 0)
    here = jnp.zeros((1, 1), F32)
    count = jnp.int32(0)
    for v in range(V):
        keep = (place // TILE < valid_ref[v, 1]) & (fr < valid_ref[v, 0])
        here = here + jnp.sum(
            jnp.where(keep, squares[v * L : (v + 1) * L], 0.0), 0, keepdims=True
        )
        count = count + valid_ref[v, 0] * valid_ref[v, 1]
    put = pltpu.make_async_copy(mixb, mixed_ref, put_sem.at[0])
    put.start()
    LS[me] = jnp.broadcast_to(here, (8, 128))
    for o in range(1, ND):
        ls(o).start()
    drain(LS.at[pl.ds(0, ND - 1)], l_r.at[0])
    loss_ref[0, 0] = jnp.sum(jnp.sum(LS[...], 0)[0:1, 0:1]) / (count.astype(F32) * TILE)

    put.wait()
    wso_x.wait_send()
    for v in range(V):
        attx(v).wait_send()
        drain(G.at[v, pl.ds(0, nch - 1), core], rs_s.at[v])
        for r in range(NR):
            line_end(functools.partial(zsend, v, r))
    line_end(zwsend)
    drain(C.at[:, :, pl.ds(0, (n_frame - 1) * tc)], a_s.at[0])
    drain(WO.at[pl.ds(0, wrows * (nch - 1)), pl.ds(0, Dh)], wg_s.at[0])
    drain(WO.at[pl.ds(0, wrows * nch), pl.ds(0, Dh)], wf_s.at[0])
    drain(LS.at[pl.ds(0, ND - 1)], l_s.at[0])


def run_kernel(timesteps, valid, tile_mask, latents, w_mod, w_sqkv, w_sout, w_tqkv, w_tout, target):
    V, L, D = latents.shape
    n_space = lax.axis_size("space")
    n_frame = lax.axis_size("frame")
    nch = n_space // 2
    ny = 2 if nch % 2 == 0 else 1
    nx = nch // ny
    NR = len(ROUNDS)
    sc, tc = w_sqkv.shape[2], w_tqkv.shape[2]
    span = n_space * L
    tl = n_frame * L // UNITS
    far = nx * ny - 1
    n1 = n_frame - 1
    dma = pltpu.SemaphoreType.DMA
    vm = pl.BlockSpec(memory_space=pltpu.VMEM)
    sm = pl.BlockSpec(memory_space=pltpu.SMEM)
    hbm = pl.BlockSpec(memory_space=pl.ANY)
    return pl.pallas_call(
        functools.partial(kernel, n_space, n_frame, nx, ny),
        out_shape=(
            jax.ShapeDtypeStruct((V, L, D), BF16),
            jax.ShapeDtypeStruct((1, 1), F32),
        ),
        in_specs=[sm, sm, vm] + [hbm] * 7,
        out_specs=(hbm, sm),
        scratch_shapes=[
            pltpu.VMEM((V, L, D), BF16),
            pltpu.VMEM((V, L, D), BF16),
            pltpu.VMEM((6, 8, D), F32),
            pltpu.VMEM((V, nch, 2, L, D), BF16),
            pltpu.VMEM((256, D), BF16),
            pltpu.VMEM((V, 2, far, L, D // 2), BF16),
            pltpu.VMEM((V, n_frame, L, D), BF16),
            pltpu.VMEM((V, L, n_frame * tc), BF16),
            pltpu.VMEM((V, L, D), BF16),
            pltpu.VMEM((n_frame * w_tout.shape[0], D), BF16),
            pltpu.VMEM(w_sqkv.shape, BF16),
            pltpu.VMEM((2,) + w_sout.shape, BF16),
            pltpu.VMEM(w_tqkv.shape, BF16),
            pltpu.VMEM((3, span, sc), BF16),
            pltpu.VMEM((V, nch, 2, L, sc), BF16),
            pltpu.VMEM((V, nch, L, sc), BF16),
            pltpu.VMEM((3, tl, tc), BF16),
            pltpu.VMEM((V, n_frame, L, tc), BF16),
            pltpu.VMEM((V, span, span), BF16),
            pltpu.VMEM((n_space * n_frame, 8, 128), F32),
            dma((V,)), dma((V, 2, far)), dma((V,)), dma((V, 2)),
            dma((V,)), dma((V, NR, 2, far)),
            dma((V, NR, 2, n1)), dma((V, NR, 2, n1)),
            dma((1,)), dma((1,)),
            dma((2, n1)), dma((2, n1)),
            dma((1,)), dma((n1, 2, far)), dma((1,)), dma((1,)),
            dma((V,)), dma((V,)), dma((1,)), dma((1,)),
            dma((1,)), dma((1,)),
            dma((6,)), dma((V,)), dma((3,)), dma((1,)),
            pltpu.VMEM((V, L, D), BF16),
        ],
        compiler_params=pltpu.CompilerParams(
            collective_id=0, has_side_effects=True, vmem_limit_bytes=61 * 1024 * 1024
        ),
        cost_estimate=pl.CostEstimate(
            flops=14_000_000_000, bytes_accessed=35_000_000, transcendentals=3_000_000
        ),
        name="block",
    )(timesteps, valid, tile_mask, latents, w_mod, w_sqkv, w_sout, w_tqkv, w_tout, target)


def shards(latents, target, timesteps, valid, tile_mask, w_mod, w_sqkv, w_sout, w_tqkv, w_tout):
    videos, frames_dev, span_dev, width = latents.shape
    shape = (videos, span_dev, width)
    mixed, loss = run_kernel(
        timesteps, valid, tile_mask, latents.reshape(shape), w_mod,
        w_sqkv, w_sout, w_tqkv, w_tout, target.reshape(shape),
    )
    return (mixed.reshape(latents.shape), loss.reshape(()))


def solution(mesh):
    return jax.shard_map(
        shards,
        mesh=mesh,
        in_specs=(
            P(None, "frame", "space", None),
            P(None, "frame", "space", None),
            P(),
            P(),
            P(),
            P(),
            P(None, None, "space"),
            P("space", None),
            P(None, None, "frame"),
            P("frame", None),
        ),
        out_specs=(P(None, "frame", "space", None), P()),
        check_vma=False,
    )
```
